32 devices in a mesh: ctx: 8 (over z, x), head: 4 (over y, core).
Axes of the slice: x: 2, y: 2, z: 4, core: 2. Of those that a mesh axis runs over, the one named last changes fastest.
Arguments:
- hidden_in: bfloat16 [1024, 4096], P('ctx'), may hold values from -30 to 30
- query_weight: bfloat16 [4096, 8192], P(None, 'head'), may hold values from -0.1875 to 0.1875
- shared_weight: bfloat16 [4096, 512], P(None, 'head'), may hold values from -0.09375 to 0.09375
- out_weight: bfloat16 [8192, 4096], P('head'), may hold values from -1 to 1
- residual: bfloat16 [1024, 4096], P(('ctx', 'head')), may hold values from -20 to 20
- norm_gain: float32 [4096], replicated, may hold values from 0.25 to 1.75
Outputs:
- residual_out: bfloat16 [1024, 4096], P(('ctx', 'head'))
- normed: bfloat16 [1024, 4096], P('ctx')
The draws below stay inside these ranges and needn't reach their ends.
All inputs are finite; a program needn't handle non-finite values.
Results may differ from the reference program's by a relative error of at most 0.0065.
The reference program's roundings to bfloat16 on the way (of `queries`, `shared`, `mixed` and `attention`) count: a program that leaves them out, or rounds other values in their place, can miss the bound.
Values may be sent and summed in bfloat16 or wider, within the bound.
No kernel may reach another device: no remote copies, remote signals or barrier semaphores. Data moves between devices by JAX's collectives and lax.ppermute only.
A program may use at most 128 MiB of HBM per device.

```python
import jax
import jax.numpy as jnp
from jax import lax

D = 4096
HEADS = 64
HD = 128
W1 = 512
W2 = 32
TOK_DEV = 128
TOKENS = 1024


def draw_hidden_in(key, part):
    noise = jnp.clip(jax.random.normal(jax.random.fold_in(key, 11), (TOKENS, D), jnp.float32), -6.0, 6.0)
    return noise.astype(jnp.bfloat16)


def draw_residual(key, part):
    noise = jax.random.normal(jax.random.fold_in(key, 21), (TOKENS, D), jnp.float32)
    return (0.5 * jnp.clip(noise, -6.0, 6.0)).astype(jnp.bfloat16)


def steps_of(own_key, extent, split, least, high):
    gain, own = 1.0, jax.random.fold_in(own_key, 6)
    for dim, blocks in split:
        draws = jnp.exp(jax.random.uniform(jax.random.fold_in(own, dim), (blocks,), jnp.float32, least / len(split), high / len(split)))
        gain = gain * jnp.repeat(draws, extent[dim] // blocks).reshape([-1 if axis == dim else 1 for axis in range(len(extent))])
    return gain


def bell_draw(rng, dims, scale, most, pieces=(), kind=jnp.bfloat16):
    values = scale * jax.random.normal(rng, dims, jnp.float32)
    if pieces:
        values = values * steps_of(rng, dims, pieces, -0.22, 0.18)
    return jnp.clip(values, -most, most).astype(kind)


def setup_inputs(seed: int = 0) -> dict:
    splits = jax.random.split(jax.random.key(seed), 7)
    hidden_in = draw_hidden_in(jax.random.fold_in(splits[6], 71), 0)
    query_weight = bell_draw(splits[1], (D, HEADS * HD), (D // 4) ** -0.5, 0.1875, ((1, 4),))
    shared_weight = bell_draw(splits[2], (D, 4 * HD), D ** -0.5, 0.09375, ((1, 4),))
    out_weight = bell_draw(splits[3], (HEADS * HD, D), (HEADS * HD // 256) ** -0.5, 1.0, ((0, 4),))
    residual = draw_residual(jax.random.fold_in(splits[6], 71), 0)
    norm_gain = jnp.clip(1.0 + 0.15 * jax.random.normal(splits[5], (D,), jnp.float32), 0.25, 1.75)
    return dict(hidden_in=hidden_in, query_weight=query_weight, shared_weight=shared_weight, out_weight=out_weight, residual=residual, norm_gain=norm_gain)


def window_mask(first, rows, spread, reach):
    query_pos = first + jnp.arange(rows, dtype=jnp.int32)[:, None, None]
    offset = jnp.arange(spread, dtype=jnp.int32)[None, :, None]
    column = jnp.arange(rows + reach, dtype=jnp.int32)[None, None, :]
    key_pos = first - reach + column
    allowed = (key_pos <= query_pos) & (key_pos > query_pos - reach) & (key_pos >= 0) & (query_pos - offset >= 0)
    return allowed

def attend_block(query, key_one, value_one, key_two, value_two, valid):
    rows = query.shape[0]
    width = query.shape[1]
    spread = key_two.shape[1]
    mixed = (query[:, None, :].astype(jnp.float32) * key_two.astype(jnp.float32)).astype(jnp.bfloat16)
    scores = jnp.dot(mixed.reshape(rows * spread, width), key_one.T, preferred_element_type=jnp.float32)
    scores = scores.reshape(rows, spread, -1) * width ** (-0.5)
    scores = jnp.where(valid, scores, -jnp.inf)
    peak = lax.optimization_barrier(jnp.max(scores, axis=(1, 2), keepdims=True))
    weights = jnp.exp(scores - peak)
    total = lax.optimization_barrier(jnp.sum(weights, axis=(1, 2)))
    blended = jnp.dot(weights.astype(jnp.bfloat16).reshape(rows * spread, -1), value_one, preferred_element_type=jnp.float32)
    blended = blended.reshape(rows, spread, width)
    return lax.optimization_barrier(jnp.sum(value_two.astype(jnp.float32) * blended, axis=1)) / total[:, None]

def reference(hidden_in, query_weight, shared_weight, out_weight, residual, norm_gain):
    queries = jnp.dot(hidden_in, query_weight, preferred_element_type=jnp.float32).astype(jnp.bfloat16)
    shared = jnp.dot(hidden_in, shared_weight, preferred_element_type=jnp.float32).astype(jnp.bfloat16)
    front_one = jnp.zeros((W1, 2 * HD), jnp.bfloat16)
    front_two = jnp.zeros((W2, 2 * HD), jnp.bfloat16)
    padded_one = jnp.concatenate([front_one, shared[:, :2 * HD]], 0)
    padded_two = jnp.concatenate([front_two, shared[:, 2 * HD:]], 0)
    block = min(128, TOK_DEV)
    heads_q = queries.reshape(TOKENS, HEADS, HD)

    def one_block(number):
        first = (number * block).astype(jnp.int32)
        window = lax.dynamic_slice_in_dim(padded_one, first, block + W1, 0)
        key_one = window[:, :HD]
        value_one = window[:, HD:]
        near = jnp.stack([lax.dynamic_slice_in_dim(padded_two, first + W2 - offset, block, 0) for offset in range(W2)], 1)
        key_two = near[:, :, :HD]
        value_two = near[:, :, HD:]
        valid = window_mask(first, block, W2, W1)
        rows_q = lax.dynamic_slice_in_dim(heads_q, first, block, 0).transpose(1, 0, 2)
        return lax.map(lambda head: attend_block(head, key_one, value_one, key_two, value_two, valid), rows_q)
    outputs = lax.map(one_block, jnp.arange(TOKENS // block, dtype=jnp.int32))
    attention = outputs.transpose(0, 2, 1, 3).reshape(TOKENS, HEADS * HD).astype(jnp.bfloat16)
    projected = jnp.dot(attention, out_weight, preferred_element_type=jnp.float32)
    residual_out = (residual.astype(jnp.float32) + projected).astype(jnp.bfloat16)
    values = residual_out.astype(jnp.float32)
    scale = lax.rsqrt(lax.optimization_barrier(jnp.mean(values * values, axis=1, keepdims=True)) + 1e-05)
    normed = (values * scale * norm_gain).astype(jnp.bfloat16)
    return (residual_out, normed)
```

```python
import functools
import math

import jax
import jax.numpy as jnp
from jax import lax
from jax.experimental import pallas as pl
from jax.experimental.pallas import tpu as pltpu
from jax.sharding import PartitionSpec as P

HD = 128
W1 = 512
W2 = 32
ROWS = 32
GROUP = 16


def from_behind(value, axis, steps):
    count = lax.axis_size(axis)
    initial, last = (max(0, -steps), min(count, count - steps))
    return lax.ppermute(value, axis, [(source, source + steps) for source in range(initial, last)])


def attention_kernel(
    place, q_ref, k1_ref, v1_ref, k2_ref, v2_ref, out_ref,
    k1_diag, v1_diag, k2_near, v2_near, keep, scores_a, scores_b, peak_a, peak_b,
):
    tokens = q_ref.shape[0]
    blocks = k1_ref.shape[0] // tokens
    pairs = q_ref.shape[1] // (2 * HD)
    chunks = tokens // ROWS
    tasks = pairs * chunks
    rate = HD ** -0.5 * math.log2(math.e)
    slab = place[0]

    k1_diag[...] = jnp.zeros(k1_diag.shape, k1_diag.dtype)
    v1_diag[...] = jnp.zeros(v1_diag.shape, v1_diag.dtype)
    for j in range(blocks):
        key = k1_ref[j * tokens:(j + 1) * tokens, :].T
        value = v1_ref[j * tokens:(j + 1) * tokens, :]
        k1_diag[j, :HD, :tokens] = key
        k1_diag[j, HD:, tokens:] = key
        v1_diag[j, :tokens, :HD] = value
        v1_diag[j, tokens:, HD:] = value
    for r in range(W2):
        k2_near[r] = k2_ref[W2 - r:W2 - r + tokens, :].astype(jnp.bfloat16)
        v2_near[r] = v2_ref[W2 - r:W2 - r + tokens, :]
    row = lax.broadcasted_iota(jnp.int32, (tokens, 2 * tokens), 0)
    col = lax.broadcasted_iota(jnp.int32, (tokens, 2 * tokens), 1) % tokens
    keep[...] = (col <= row).astype(jnp.float32).astype(jnp.bfloat16)

    def twice(x):
        return jnp.concatenate([x, x], axis=-1)

    def split(task):
        pair, chunk = task // chunks, task % chunks
        return pl.multiple_of(chunk * ROWS, ROWS), pl.multiple_of(pair * 2 * HD, 2 * HD)

    def score(task, group, scores, full, peak):
        first, lane = split(task)
        query = q_ref[pl.ds(first, ROWS), pl.ds(lane, 2 * HD)]
        near = k2_near[group * GROUP:(group + 1) * GROUP, pl.ds(first, ROWS), :]
        mixed = (query[None] * twice(near)).reshape(GROUP * ROWS, 2 * HD)
        row = first + lax.broadcasted_iota(jnp.int32, (ROWS, 2 * tokens), 0)
        col = lax.broadcasted_iota(jnp.int32, (ROWS, 2 * tokens), 1) % tokens
        recent = (col <= row)[None]
        last = jnp.dot(mixed, k1_diag[blocks - 1], preferred_element_type=jnp.float32)
        last = last.reshape(GROUP, ROWS, 2 * tokens)
        if not full:
            offset = group * GROUP + lax.broadcasted_iota(jnp.int32, (GROUP, ROWS, 1), 0)
            place_row = slab * tokens + first + lax.broadcasted_iota(jnp.int32, (GROUP, ROWS, 1), 1)
            bias = jnp.where(place_row >= offset, 0.0, -jnp.inf)
            last = last + bias
        for j in range(blocks - 1):
            part = jnp.dot(mixed, k1_diag[j], preferred_element_type=jnp.float32)
            part = part.reshape(GROUP, ROWS, 2 * tokens)
            if not full:
                part = part + jnp.where(slab + j >= blocks - 1, bias, -jnp.inf)
            if j == 0:
                part = jnp.where(recent, last, part)
            scores[group, j] = part
            high = jnp.max(part, axis=0)
            peak = high if peak is None else jnp.maximum(peak, high)
        return peak

    def finish_peak(peak):
        left = jnp.max(peak[:, :tokens], axis=1, keepdims=True)
        right = jnp.max(peak[:, tokens:], axis=1, keepdims=True)
        return jnp.concatenate(
            [jnp.broadcast_to(left, (ROWS, tokens)), jnp.broadcast_to(right, (ROWS, tokens))], axis=1
        ) * rate

    def blend(task, group, scores, peak, acc, total):
        first, _ = split(task)
        mask = keep[pl.ds(first, ROWS), :][None]
        blended = None
        for j in range(blocks - 1):
            weights = jnp.exp2(scores[group, j] * rate - peak[None])
            part = jnp.sum(weights, axis=0)
            total = part if total is None else total + part
            weights = weights.astype(jnp.bfloat16)
            if j == 0:
                late = weights * mask
                weights = weights - late
                blended = jnp.dot(
                    late.reshape(GROUP * ROWS, 2 * tokens), v1_diag[blocks - 1],
                    preferred_element_type=jnp.float32,
                )
            blended = blended + jnp.dot(
                weights.reshape(GROUP * ROWS, 2 * tokens), v1_diag[j],
                preferred_element_type=jnp.float32,
            )
        near = v2_near[group * GROUP:(group + 1) * GROUP, pl.ds(first, ROWS), :]
        part = jnp.sum(twice(near) * blended.reshape(GROUP, ROWS, 2 * HD), axis=0)
        return (part if acc is None else acc + part), total

    def store(task, acc, total):
        first, lane = split(task)
        left = jnp.sum(total[:, :tokens], axis=1, keepdims=True)
        right = jnp.sum(total[:, tokens:], axis=1, keepdims=True)
        out = jnp.concatenate([acc[:, :HD] / left, acc[:, HD:] / right], axis=1)
        out_ref[pl.ds(first, ROWS), pl.ds(lane, 2 * HD)] = out.astype(out_ref.dtype)

    def step(task, ahead, here, here_peak, there, there_peak, full):
        peak_now = here_peak[...]
        acc = total = peak = None
        for group in range(W2 // GROUP):
            peak = score(ahead, group, there, full, peak)
            acc, total = blend(task, group, here, peak_now, acc, total)
        there_peak[...] = finish_peak(peak)
        store(task, acc, total)

    def run(full):
        peak = None
        for group in range(W2 // GROUP):
            peak = score(0, group, scores_a, full, peak)
        peak_a[...] = finish_peak(peak)

        def two(index, _):
            task = 2 * index
            step(task, task + 1, scores_a, peak_a, scores_b, peak_b, full)
            step(task + 1, jnp.minimum(task + 2, tasks - 1), scores_b, peak_b, scores_a, peak_a, full)
            return 0

        lax.fori_loop(0, tasks // 2, two, 0)

    @pl.when(slab >= blocks - 1)
    def _():
        run(True)

    @pl.when(slab < blocks - 1)
    def _():
        run(False)


def attention_of(place, queries, extended_one, extended_two):
    tokens, width = queries.shape
    blocks = extended_one.shape[0] // tokens
    vmem = pl.BlockSpec(memory_space=pltpu.VMEM)
    return pl.pallas_call(
        attention_kernel,
        out_shape=jax.ShapeDtypeStruct((tokens, width), jnp.bfloat16),
        in_specs=[pl.BlockSpec(memory_space=pltpu.SMEM)] + [vmem] * 5,
        out_specs=vmem,
        scratch_shapes=[
            pltpu.VMEM((blocks, 2 * HD, 2 * tokens), jnp.bfloat16),
            pltpu.VMEM((blocks, 2 * tokens, 2 * HD), jnp.bfloat16),
            pltpu.VMEM((W2, tokens, HD), jnp.bfloat16),
            pltpu.VMEM((W2, tokens, HD), jnp.float32),
            pltpu.VMEM((tokens, 2 * tokens), jnp.bfloat16),
        ]
        + [pltpu.VMEM((W2 // GROUP, blocks - 1, GROUP, ROWS, 2 * tokens), jnp.float32)] * 2
        + [pltpu.VMEM((ROWS, 2 * tokens), jnp.float32)] * 2,
        compiler_params=pltpu.CompilerParams(vmem_limit_bytes=48 * 1024 * 1024),
        name="attention",
    )(
        place,
        queries,
        extended_one[:, :HD],
        extended_one[:, HD:],
        extended_two[:, :HD].astype(jnp.float32),
        extended_two[:, HD:].astype(jnp.float32),
    )


def body(hidden_in, query_weight, shared_weight, out_weight, residual, norm_gain):
    tokens = hidden_in.shape[0]
    queries = jnp.dot(hidden_in, query_weight, preferred_element_type=jnp.float32).astype(
        jnp.bfloat16
    )
    local_part = jnp.dot(hidden_in, shared_weight, preferred_element_type=jnp.float32).astype(
        jnp.bfloat16
    )
    shared = lax.all_gather(local_part, "head", axis=1, tiled=True)
    first_pair = shared[:, : 2 * HD]
    second_pair = shared[:, 2 * HD :]
    reach = (W1 + tokens - 1) // tokens
    earlier, rim = from_behind((first_pair, second_pair[tokens - W2 :]), "ctx", 1)
    pieces = [earlier]
    for distance in range(2, reach + 1):
        pieces.append(from_behind(first_pair, "ctx", distance))
    extended_one = jnp.concatenate(pieces[::-1] + [first_pair], 0)
    extended_two = jnp.concatenate([rim, second_pair], 0)
    place = lax.axis_index("ctx").astype(jnp.int32).reshape(1)
    attention = attention_of(place, queries, extended_one, extended_two)
    summed = lax.psum_scatter(
        jnp.dot(attention, out_weight, preferred_element_type=jnp.float32),
        "head",
        scatter_dimension=0,
        tiled=True,
    )
    residual_out = (residual.astype(jnp.float32) + summed).astype(jnp.bfloat16)
    values = residual_out.astype(jnp.float32)
    scale = lax.rsqrt(jnp.mean(values * values, axis=1, keepdims=True) + 1e-05)
    normed_local = (values * scale * norm_gain).astype(jnp.bfloat16)
    normed = lax.all_gather(normed_local, "head", axis=0, tiled=True)
    return (residual_out, normed)


def solution(mesh):
    in_specs = (
        P("ctx", None),
        P(None, "head"),
        P(None, "head"),
        P("head", None),
        P(("ctx", "head"), None),
        P(),
    )
    out_specs = (P(("ctx", "head"), None), P("ctx", None))
    return jax.shard_map(body, mesh=mesh, in_specs=in_specs, out_specs=out_specs, check_vma=False)
```

```python
import functools
import math

import jax
import jax.numpy as jnp
from jax import lax
from jax.experimental import pallas as pl
from jax.experimental.pallas import tpu as pltpu
from jax.sharding import PartitionSpec as P

HD = 128
W1 = 512
W2 = 32
ROWS = 32
GROUP = 16


def from_behind(value, axis, steps):
    count = lax.axis_size(axis)
    initial, last = (max(0, -steps), min(count, count - steps))
    return lax.ppermute(value, axis, [(source, source + steps) for source in range(initial, last)])


def swap(value, axis, bit):
    count = lax.axis_size(axis)
    return lax.ppermute(value, axis, [(source, source ^ (1 << bit)) for source in range(count)])


def pick(value, place, dim):
    return lax.dynamic_index_in_dim(value, place, dim, keepdims=False)


def sum_to_owner(value, axis):
    count = lax.axis_size(axis)
    if count & (count - 1):
        return lax.psum_scatter(value, axis, scatter_dimension=0, tiled=True)
    place = lax.axis_index(axis)
    value = value.reshape(count, value.shape[0] // count, value.shape[1])
    for bit in range(count.bit_length() - 1):
        value = value.reshape(value.shape[0] // 2, 2, *value.shape[1:])
        mine = (place >> bit) & 1
        value = pick(value, mine, 1) + swap(
            pick(value, 1 - mine, 1).astype(jnp.bfloat16), axis, bit
        ).astype(jnp.float32)
    return value[0]


def share_rows(value, axis):
    count = lax.axis_size(axis)
    if count & (count - 1):
        return lax.all_gather(value, axis, axis=0, tiled=True)
    place = lax.axis_index(axis)
    rows, width = value.shape
    value = value[None]
    for bit in reversed(range(count.bit_length() - 1)):
        mine = (place >> bit) & 1
        other = swap(value, axis, bit)
        value = jnp.where(mine == 0, jnp.stack([value, other], 1), jnp.stack([other, value], 1))
        value = value.reshape(-1, rows, width)
    return value.reshape(-1, width)


def attention_kernel(
    place, q_ref, k1_ref, v1_ref, k2_ref, v2_ref, out_ref,
    k1_diag, v1_diag, k2_near, v2_near, keep, scores_a, scores_b, peak_a, peak_b,
):
    tokens = q_ref.shape[0]
    blocks = k1_ref.shape[0] // tokens
    pairs = q_ref.shape[1] // (2 * HD)
    chunks = tokens // ROWS
    tasks = pairs * chunks
    rate = HD ** -0.5 * math.log2(math.e)
    slab = place[0]

    k1_diag[...] = jnp.zeros(k1_diag.shape, k1_diag.dtype)
    v1_diag[...] = jnp.zeros(v1_diag.shape, v1_diag.dtype)
    for j in range(blocks):
        key = k1_ref[j * tokens:(j + 1) * tokens, :].T
        value = v1_ref[j * tokens:(j + 1) * tokens, :]
        k1_diag[j, :HD, :tokens] = key
        k1_diag[j, HD:, tokens:] = key
        v1_diag[j, :tokens, :HD] = value
        v1_diag[j, tokens:, HD:] = value
    for r in range(W2):
        k2_near[r] = k2_ref[W2 - r:W2 - r + tokens, :].astype(jnp.bfloat16)
        v2_near[r] = v2_ref[W2 - r:W2 - r + tokens, :]
    row = lax.broadcasted_iota(jnp.int32, (tokens, 2 * tokens), 0)
    col = lax.broadcasted_iota(jnp.int32, (tokens, 2 * tokens), 1) % tokens
    keep[...] = (col <= row).astype(jnp.float32).astype(jnp.bfloat16)

    def twice(x):
        return jnp.concatenate([x, x], axis=-1)

    def split(task):
        pair, chunk = task // chunks, task % chunks
        return pl.multiple_of(chunk * ROWS, ROWS), pl.multiple_of(pair * 2 * HD, 2 * HD)

    def score(task, group, scores, full, peak):
        first, lane = split(task)
        query = q_ref[pl.ds(first, ROWS), pl.ds(lane, 2 * HD)]
        near = k2_near[group * GROUP:(group + 1) * GROUP, pl.ds(first, ROWS), :]
        mixed = (query[None] * twice(near)).reshape(GROUP * ROWS, 2 * HD)
        row = first + lax.broadcasted_iota(jnp.int32, (ROWS, 2 * tokens), 0)
        col = lax.broadcasted_iota(jnp.int32, (ROWS, 2 * tokens), 1) % tokens
        recent = (col <= row)[None]
        last = jnp.dot(mixed, k1_diag[blocks - 1], preferred_element_type=jnp.float32)
        last = last.reshape(GROUP, ROWS, 2 * tokens)
        if not full:
            offset = group * GROUP + lax.broadcasted_iota(jnp.int32, (GROUP, ROWS, 1), 0)
            place_row = slab * tokens + first + lax.broadcasted_iota(jnp.int32, (GROUP, ROWS, 1), 1)
            bias = jnp.where(place_row >= offset, 0.0, -jnp.inf)
            last = last + bias
        for j in range(blocks - 1):
            part = jnp.dot(mixed, k1_diag[j], preferred_element_type=jnp.float32)
            part = part.reshape(GROUP, ROWS, 2 * tokens)
            if not full:
                part = part + jnp.where(slab + j >= blocks - 1, bias, -jnp.inf)
            if j == 0:
                part = jnp.where(recent, last, part)
            scores[group, j] = part
            high = jnp.max(part, axis=0)
            peak = high if peak is None else jnp.maximum(peak, high)
        return peak

    def finish_peak(peak):
        left = jnp.max(peak[:, :tokens], axis=1, keepdims=True)
        right = jnp.max(peak[:, tokens:], axis=1, keepdims=True)
        return jnp.concatenate(
            [jnp.broadcast_to(left, (ROWS, tokens)), jnp.broadcast_to(right, (ROWS, tokens))], axis=1
        ) * rate

    def blend(task, group, scores, peak, acc, total):
        first, _ = split(task)
        mask = keep[pl.ds(first, ROWS), :][None]
        blended = None
        for j in range(blocks - 1):
            weights = jnp.exp2(scores[group, j] * rate - peak[None])
            part = jnp.sum(weights, axis=0)
            total = part if total is None else total + part
            weights = weights.astype(jnp.bfloat16)
            if j == 0:
                late = weights * mask
                weights = weights - late
                blended = jnp.dot(
                    late.reshape(GROUP * ROWS, 2 * tokens), v1_diag[blocks - 1],
                    preferred_element_type=jnp.float32,
                )
            blended = blended + jnp.dot(
                weights.reshape(GROUP * ROWS, 2 * tokens), v1_diag[j],
                preferred_element_type=jnp.float32,
            )
        near = v2_near[group * GROUP:(group + 1) * GROUP, pl.ds(first, ROWS), :]
        part = jnp.sum(twice(near) * blended.reshape(GROUP, ROWS, 2 * HD), axis=0)
        return (part if acc is None else acc + part), total

    def store(task, acc, total):
        first, lane = split(task)
        left = jnp.sum(total[:, :tokens], axis=1, keepdims=True)
        right = jnp.sum(total[:, tokens:], axis=1, keepdims=True)
        out = jnp.concatenate([acc[:, :HD] / left, acc[:, HD:] / right], axis=1)
        out_ref[pl.ds(first, ROWS), pl.ds(lane, 2 * HD)] = out.astype(out_ref.dtype)

    def step(task, ahead, here, here_peak, there, there_peak, full):
        peak_now = here_peak[...]
        acc = total = peak = None
        for group in range(W2 // GROUP):
            peak = score(ahead, group, there, full, peak)
            acc, total = blend(task, group, here, peak_now, acc, total)
        there_peak[...] = finish_peak(peak)
        store(task, acc, total)

    def run(full):
        peak = None
        for group in range(W2 // GROUP):
            peak = score(0, group, scores_a, full, peak)
        peak_a[...] = finish_peak(peak)

        def two(index, _):
            task = 2 * index
            step(task, task + 1, scores_a, peak_a, scores_b, peak_b, full)
            step(task + 1, jnp.minimum(task + 2, tasks - 1), scores_b, peak_b, scores_a, peak_a, full)
            return 0

        lax.fori_loop(0, tasks // 2, two, 0)

    @pl.when(slab >= blocks - 1)
    def _():
        run(True)

    @pl.when(slab < blocks - 1)
    def _():
        run(False)


def attention_of(place, queries, extended_one, extended_two):
    tokens, width = queries.shape
    blocks = extended_one.shape[0] // tokens
    vmem = pl.BlockSpec(memory_space=pltpu.VMEM)
    return pl.pallas_call(
        attention_kernel,
        out_shape=jax.ShapeDtypeStruct((tokens, width), jnp.bfloat16),
        in_specs=[pl.BlockSpec(memory_space=pltpu.SMEM)] + [vmem] * 5,
        out_specs=vmem,
        scratch_shapes=[
            pltpu.VMEM((blocks, 2 * HD, 2 * tokens), jnp.bfloat16),
            pltpu.VMEM((blocks, 2 * tokens, 2 * HD), jnp.bfloat16),
            pltpu.VMEM((W2, tokens, HD), jnp.bfloat16),
            pltpu.VMEM((W2, tokens, HD), jnp.float32),
            pltpu.VMEM((tokens, 2 * tokens), jnp.bfloat16),
        ]
        + [pltpu.VMEM((W2 // GROUP, blocks - 1, GROUP, ROWS, 2 * tokens), jnp.float32)] * 2
        + [pltpu.VMEM((ROWS, 2 * tokens), jnp.float32)] * 2,
        compiler_params=pltpu.CompilerParams(vmem_limit_bytes=48 * 1024 * 1024),
        name="attention",
    )(
        place,
        queries,
        extended_one[:, :HD],
        extended_one[:, HD:],
        extended_two[:, :HD].astype(jnp.float32),
        extended_two[:, HD:].astype(jnp.float32),
    )


def body(hidden_in, query_weight, shared_weight, out_weight, residual, norm_gain):
    tokens = hidden_in.shape[0]
    queries = jnp.dot(hidden_in, query_weight, preferred_element_type=jnp.float32).astype(
        jnp.bfloat16
    )
    local_part = jnp.dot(hidden_in, shared_weight, preferred_element_type=jnp.float32).astype(
        jnp.bfloat16
    )
    shared = lax.all_gather(local_part, "head", axis=1, tiled=True)
    first_pair = shared[:, : 2 * HD]
    second_pair = shared[:, 2 * HD :]
    reach = (W1 + tokens - 1) // tokens
    earlier, rim = from_behind((first_pair, second_pair[tokens - W2 :]), "ctx", 1)
    pieces = [earlier]
    for distance in range(2, reach + 1):
        pieces.append(from_behind(first_pair, "ctx", distance))
    extended_one = jnp.concatenate(pieces[::-1] + [first_pair], 0)
    extended_two = jnp.concatenate([rim, second_pair], 0)
    place = lax.axis_index("ctx").astype(jnp.int32).reshape(1)
    attention = attention_of(place, queries, extended_one, extended_two)
    summed = sum_to_owner(
        jnp.dot(attention, out_weight, preferred_element_type=jnp.float32), "head"
    )
    residual_out = (residual.astype(jnp.float32) + summed).astype(jnp.bfloat16)
    values = residual_out.astype(jnp.float32)
    scale = lax.rsqrt(jnp.mean(values * values, axis=1, keepdims=True) + 1e-05)
    normed_local = (values * scale * norm_gain).astype(jnp.bfloat16)
    normed = share_rows(normed_local, "head")
    return (residual_out, normed)


def solution(mesh):
    in_specs = (
        P("ctx", None),
        P(None, "head"),
        P(None, "head"),
        P("head", None),
        P(("ctx", "head"), None),
        P(),
    )
    out_specs = (P(("ctx", "head"), None), P("ctx", None))
    return jax.shard_map(body, mesh=mesh, in_specs=in_specs, out_specs=out_specs, check_vma=False)
```

```python
import math

import jax
import jax.numpy as jnp
from jax import lax
from jax.experimental import pallas as pl
from jax.experimental.pallas import tpu as pltpu
from jax.sharding import PartitionSpec as P

HD = 128
W1 = 512
W2 = 32
GROUP = 2


def from_behind(value, axis, steps):
    count = lax.axis_size(axis)
    initial, last = (max(0, -steps), min(count, count - steps))
    return lax.ppermute(value, axis, [(source, source + steps) for source in range(initial, last)])


def swap(value, axis, bit):
    count = lax.axis_size(axis)
    return lax.ppermute(value, axis, [(source, source ^ (1 << bit)) for source in range(count)])


def pick(value, place, dim):
    return lax.dynamic_index_in_dim(value, place, dim, keepdims=False)


def sum_to_owner(value, axis):
    count = lax.axis_size(axis)
    if count & (count - 1):
        return lax.psum_scatter(value, axis, scatter_dimension=0, tiled=True)
    place = lax.axis_index(axis)
    value = value.reshape(count, value.shape[0] // count, value.shape[1])
    for bit in range(count.bit_length() - 1):
        value = value.reshape(value.shape[0] // 2, 2, *value.shape[1:])
        mine = (place >> bit) & 1
        value = pick(value, mine, 1) + swap(
            pick(value, 1 - mine, 1).astype(jnp.bfloat16), axis, bit
        ).astype(jnp.float32)
    return value[0]


def share_rows(value, axis):
    count = lax.axis_size(axis)
    if count & (count - 1):
        return lax.all_gather(value, axis, axis=0, tiled=True)
    place = lax.axis_index(axis)
    rows, width = value.shape
    value = value[None]
    for bit in reversed(range(count.bit_length() - 1)):
        mine = (place >> bit) & 1
        other = swap(value, axis, bit)
        value = jnp.where(mine == 0, jnp.stack([value, other], 1), jnp.stack([other, value], 1))
        value = value.reshape(-1, rows, width)
    return value.reshape(-1, width)


def attention_kernel(
    place, q_ref, k1_ref, v1_ref, k2_ref, v2_ref, out_ref,
    query, last_key, first_key, key_diag, value_diag, column, order, result, scores, peaks,
):
    tokens = q_ref.shape[0]
    blocks = k1_ref.shape[0] // tokens
    pairs = q_ref.shape[1] // (2 * HD)
    lines = query.shape[1]
    rows = lines * W2
    rate = HD ** -0.5 * math.log2(math.e)
    slab = place[0]

    def twice(x):
        return jnp.concatenate([x, x], axis=-1)

    def diag(x):
        zero = jnp.zeros_like(x)
        return jnp.concatenate(
            [jnp.concatenate([x, zero], axis=1), jnp.concatenate([zero, x], axis=1)], axis=0
        )

    if lines > pairs:
        query[...] = jnp.zeros(query.shape, query.dtype)
    for pair in range(pairs):
        query[:, pair, :] = q_ref[:, pair * 2 * HD:(pair + 1) * 2 * HD].astype(jnp.float32)
    first_key[...] = k1_ref[:tokens, :].T
    last_key[...] = k1_ref[(blocks - 1) * tokens:, :].T
    for j in range(blocks - 1):
        value_diag[j] = diag(v1_ref[j * tokens:(j + 1) * tokens, :])
        if j > 0:
            key_diag[j - 1] = diag(k1_ref[j * tokens:(j + 1) * tokens, :].T)
    order[...] = lax.broadcasted_iota(jnp.int32, order.shape, 0).astype(jnp.float32).astype(order.dtype)
    column[...] = lax.broadcasted_iota(jnp.int32, column.shape, 1).astype(jnp.float32).astype(column.dtype)

    def score(position, slot, full):
        line = query[position]
        line = jnp.concatenate([line] * (16 // lines), axis=0).astype(jnp.bfloat16)
        mixed = []
        for start in range(0, W2, 16 // lines):
            near = [
                jnp.broadcast_to(k2_ref[pl.ds(position + 1 + start + step, 1), :], (lines, HD))
                for step in range(16 // lines)
            ]
            mixed.append(line * twice(jnp.concatenate(near, axis=0).astype(jnp.bfloat16)))
        mixed = jnp.concatenate(mixed, axis=0)
        here = jnp.broadcast_to(position, (16, tokens)).astype(jnp.float32).astype(jnp.bfloat16)
        late = jnp.concatenate([column[...] <= here] * (HD // 16), axis=0)
        if not full:
            shown = lax.broadcasted_iota(jnp.int32, (W2, 1, 1), 0) + (slab * tokens + position - W2 + 1)
            shown = jnp.where(shown >= 0, 0.0, -jnp.inf)
            allowed = lax.broadcasted_iota(jnp.int32, (1, 2 * tokens), 1) % tokens <= position
            allowed = jnp.where(allowed, 0.0, -jnp.inf)
        peak = None
        for j in range(blocks - 1):
            if j == 0:
                weights = diag(jnp.where(late, last_key[...], first_key[...]))
            else:
                weights = key_diag[j - 1]
            part = jnp.dot(mixed, weights, preferred_element_type=jnp.float32)
            if not full:
                bias = jnp.where(slab + j >= blocks - 1, 0.0, -jnp.inf)
                bias = jnp.maximum(bias, allowed) if j == 0 else jnp.broadcast_to(bias, allowed.shape)
                part = (part.reshape(W2, lines, 2 * tokens) + (shown + bias[None])).reshape(part.shape)
            scores[slot, j] = part
            high = jnp.max(part.reshape(W2, lines, 2 * tokens), axis=0)
            peak = high if peak is None else jnp.maximum(peak, high)
        left = jnp.max(peak[:, :tokens], axis=1, keepdims=True) * rate
        right = jnp.max(peak[:, tokens:], axis=1, keepdims=True) * rate
        peaks[slot] = jnp.concatenate(
            [jnp.broadcast_to(left, (lines, tokens)), jnp.broadcast_to(right, (lines, tokens))], axis=1
        )

    def blend(position, slot):
        base = pl.multiple_of(position // 16 * 16, 16)
        far = pl.multiple_of((blocks - 1) * tokens + base, 16)
        late = order[...] <= jnp.broadcast_to(position - base, (16, HD)).astype(jnp.float32).astype(jnp.bfloat16)
        value = jnp.where(late, v1_ref[pl.ds(far, 16), :], v1_ref[pl.ds(base, 16), :])
        value_diag[0, pl.ds(base, 16), :HD] = value
        value_diag[0, pl.ds(pl.multiple_of(tokens + base, 16), 16), HD:] = value
        peak = peaks[slot][None]
        blended = total = None
        for j in range(blocks - 1):
            part = scores[slot, j].reshape(W2, lines, 2 * tokens)
            part = jnp.exp2(part * rate - peak)
            add = jnp.sum(part, axis=0)
            total = add if total is None else total + add
            part = jnp.dot(
                part.reshape(rows, 2 * tokens).astype(jnp.bfloat16), value_diag[j],
                preferred_element_type=jnp.float32,
            )
            blended = part if blended is None else blended + part
        acc = None
        for step in range(W2):
            near = jnp.broadcast_to(v2_ref[pl.ds(position + 1 + step, 1), :], (lines, HD))
            part = twice(near) * blended[step * lines:(step + 1) * lines]
            acc = part if acc is None else acc + part
        left = jnp.sum(total[:, :tokens], axis=1, keepdims=True)
        right = jnp.sum(total[:, tokens:], axis=1, keepdims=True)
        result[position] = jnp.concatenate([acc[:, :HD] / left, acc[:, HD:] / right], axis=1)

    def run(full):
        for step in range(GROUP):
            score(step, step, full)

        def trip(index, _):
            for half in range(2):
                first = (2 * index + half) * GROUP
                for step in range(GROUP):
                    ahead = jnp.minimum(first + GROUP + step, tokens - 1)
                    score(ahead, (1 - half) * GROUP + step, full)
                    blend(first + step, half * GROUP + step)
            return 0

        lax.fori_loop(0, tokens // (2 * GROUP), trip, 0)

    @pl.when(slab >= blocks - 1)
    def _():
        run(True)

    @pl.when(slab < blocks - 1)
    def _():
        run(False)

    for pair in range(pairs):
        out_ref[:, pair * 2 * HD:(pair + 1) * 2 * HD] = result[:, pair, :].astype(out_ref.dtype)


def attention_of(place, queries, extended_one, extended_two):
    tokens, width = queries.shape
    blocks = extended_one.shape[0] // tokens
    pairs = width // (2 * HD)
    lines = -(-pairs // 8) * 8
    rows = lines * W2
    vmem = pl.BlockSpec(memory_space=pltpu.VMEM)
    return pl.pallas_call(
        attention_kernel,
        out_shape=jax.ShapeDtypeStruct((tokens, width), jnp.bfloat16),
        in_specs=[pl.BlockSpec(memory_space=pltpu.SMEM)] + [vmem] * 5,
        out_specs=vmem,
        scratch_shapes=[
            pltpu.VMEM((tokens, lines, 2 * HD), jnp.float32),
            pltpu.VMEM((HD, tokens), jnp.bfloat16),
            pltpu.VMEM((HD, tokens), jnp.bfloat16),
            pltpu.VMEM((blocks - 2, 2 * HD, 2 * tokens), jnp.bfloat16),
            pltpu.VMEM((blocks - 1, 2 * tokens, 2 * HD), jnp.bfloat16),
            pltpu.VMEM((16, tokens), jnp.bfloat16),
            pltpu.VMEM((16, HD), jnp.bfloat16),
            pltpu.VMEM((tokens, lines, 2 * HD), jnp.float32),
            pltpu.VMEM((2 * GROUP, blocks - 1, rows, 2 * tokens), jnp.float32),
            pltpu.VMEM((2 * GROUP, lines, 2 * tokens), jnp.float32),
        ],
        compiler_params=pltpu.CompilerParams(vmem_limit_bytes=48 * 1024 * 1024),
        name="attention",
    )(
        place,
        queries,
        extended_one[:, :HD],
        extended_one[:, HD:],
        extended_two[:, :HD].astype(jnp.float32),
        extended_two[:, HD:].astype(jnp.float32),
    )


def body(hidden_in, query_weight, shared_weight, out_weight, residual, norm_gain):
    tokens = hidden_in.shape[0]
    queries = jnp.dot(hidden_in, query_weight, preferred_element_type=jnp.float32).astype(
        jnp.bfloat16
    )
    local_part = jnp.dot(hidden_in, shared_weight, preferred_element_type=jnp.float32).astype(
        jnp.bfloat16
    )
    shared = lax.all_gather(local_part, "head", axis=1, tiled=True)
    first_pair = shared[:, : 2 * HD]
    second_pair = shared[:, 2 * HD :]
    reach = (W1 + tokens - 1) // tokens
    earlier, rim = from_behind((first_pair, second_pair[tokens - W2 :]), "ctx", 1)
    pieces = [earlier]
    for distance in range(2, reach + 1):
        pieces.append(from_behind(first_pair, "ctx", distance))
    extended_one = jnp.concatenate(pieces[::-1] + [first_pair], 0)
    extended_two = jnp.concatenate([rim, second_pair], 0)
    place = lax.axis_index("ctx").astype(jnp.int32).reshape(1)
    attention = attention_of(place, queries, extended_one, extended_two)
    summed = sum_to_owner(
        jnp.dot(attention, out_weight, preferred_element_type=jnp.float32), "head"
    )
    residual_out = (residual.astype(jnp.float32) + summed).astype(jnp.bfloat16)
    values = residual_out.astype(jnp.float32)
    scale = lax.rsqrt(jnp.mean(values * values, axis=1, keepdims=True) + 1e-05)
    normed_local = (values * scale * norm_gain).astype(jnp.bfloat16)
    normed = share_rows(normed_local, "head")
    return (residual_out, normed)


def solution(mesh):
    in_specs = (
        P("ctx", None),
        P(None, "head"),
        P(None, "head"),
        P("head", None),
        P(("ctx", "head"), None),
        P(),
    )
    out_specs = (P(("ctx", "head"), None), P("ctx", None))
    return jax.shard_map(body, mesh=mesh, in_specs=in_specs, out_specs=out_specs, check_vma=False)
```

```python
import functools
import math

import jax
import jax.numpy as jnp
from jax import lax
from jax.experimental import pallas as pl
from jax.experimental.pallas import tpu as pltpu
from jax.sharding import PartitionSpec as P

HD = 128
W1 = 512
W2 = 32
GROUP = 2
PIECES = 4


def from_behind(value, axis, steps):
    count = lax.axis_size(axis)
    initial, last = (max(0, -steps), min(count, count - steps))
    return lax.ppermute(value, axis, [(source, source + steps) for source in range(initial, last)])


def swap(value, axis, bit):
    count = lax.axis_size(axis)
    return lax.ppermute(value, axis, [(source, source ^ (1 << bit)) for source in range(count)])


def pick(value, place, dim):
    return lax.dynamic_index_in_dim(value, place, dim, keepdims=False)


def sum_to_owner(value, axis):
    count = lax.axis_size(axis)
    if count & (count - 1):
        return lax.psum_scatter(value, axis, scatter_dimension=0, tiled=True)
    place = lax.axis_index(axis)
    value = value.reshape(count, value.shape[0] // count, value.shape[1])
    for bit in range(count.bit_length() - 1):
        value = value.reshape(value.shape[0] // 2, 2, *value.shape[1:])
        mine = (place >> bit) & 1
        value = pick(value, mine, 1) + swap(
            pick(value, 1 - mine, 1).astype(jnp.bfloat16), axis, bit
        ).astype(jnp.float32)
    return value[0]


def share_rows(value, axis):
    count = lax.axis_size(axis)
    if count & (count - 1):
        return lax.all_gather(value, axis, axis=0, tiled=True)
    place = lax.axis_index(axis)
    rows, width = value.shape
    value = value[None]
    for bit in reversed(range(count.bit_length() - 1)):
        mine = (place >> bit) & 1
        other = swap(value, axis, bit)
        value = jnp.where(mine == 0, jnp.stack([value, other], 1), jnp.stack([other, value], 1))
        value = value.reshape(-1, rows, width)
    return value.reshape(-1, width)


def gather_columns(value):
    count = value.shape[0] * value.shape[1]
    return value.reshape(count, *value.shape[2:]).transpose(1, 0, 2).reshape(value.shape[2], -1)


def place_pair(mine, value, other, dim):
    return jnp.where(
        mine == 0, jnp.concatenate([value, other], dim), jnp.concatenate([other, value], dim)
    )


def simple_window(local_part):
    tokens = local_part.shape[0]
    shared = lax.all_gather(local_part, "head", axis=1, tiled=True)
    first_pair = shared[:, : 2 * HD]
    second_pair = shared[:, 2 * HD :]
    reach = W1 // tokens
    earlier, rim = from_behind((first_pair, second_pair[tokens - W2 :]), "ctx", 1)
    pieces = [earlier]
    for distance in range(2, reach + 1):
        pieces.append(from_behind(first_pair, "ctx", distance))
    one = jnp.concatenate(pieces[::-1] + [first_pair], 0)
    two = jnp.concatenate([rim, second_pair], 0)
    return one[:, :HD], one[:, HD:], two[:, :HD], two[:, HD:]


def window_of(local_part, source, work):
    tokens = local_part.shape[0]
    heads = lax.axis_size("head")
    slab = lax.axis_index("ctx")
    done = []

    def beside(value):
        nonlocal source
        if work:
            value, source = lax.optimization_barrier((value, source))
            done.append(work.pop(0)(source))
        return value

    short = (
        heads & (heads - 1) == 0 and heads >= 4 and lax.axis_size("ctx") % 2 == 0 and W1 == 4 * tokens
    )
    if not short:
        out = simple_window(local_part)
        while work:
            done.append(work.pop(0)(source))
        return out, jnp.int32(0), done

    place = lax.axis_index("head")
    done.append(work.pop(0)(source))
    value = local_part[None]
    for bit in reversed(range(1, heads.bit_length() - 1)):
        other = swap(value, "head", bit)
        value = jnp.stack(
            [jnp.where((place >> bit) & 1 == 0, value, other), jnp.where((place >> bit) & 1 == 0, other, value)], 1
        )
        value = value.reshape(-1, *local_part.shape)
    half = value.shape[0] // 2
    first, second = value[:half], value[half:]

    odd = slab & 1
    rim = second[:, tokens - W2 :]
    other = swap(beside(jnp.concatenate([first, rim], 1)), "ctx", 0)
    other, other_rim = other[:, :tokens], other[:, tokens:]
    pair = place_pair(odd, first, other, 1)
    pair_rim = jnp.where(odd == 0, other_rim, rim)
    behind = from_behind(beside(jnp.concatenate([pair, pair_rim], 1)), "ctx", 2)
    behind, behind_rim = behind[:, : 2 * tokens], behind[:, 2 * tokens :]
    further = from_behind(beside(behind), "ctx", 2)
    rim = jnp.where(odd == 0, behind_rim, other_rim)
    value = jnp.concatenate([further, behind, pair, rim, second], 1)
    other = swap(beside(value), "head", 0)
    value = place_pair(place & 1, value[:, None], other[:, None], 1)
    one, two = value[:, :, : 6 * tokens], value[:, :, 6 * tokens :]
    one, two = gather_columns(one), gather_columns(two)
    while work:
        done.append(work.pop(0)(source))
    return (one[:, :HD], one[:, HD:], two[:, :HD], two[:, HD:]), odd, done


def attention_kernel(
    place, q_ref, k1_ref, v1_ref, k2_ref, v2_ref, out_ref,
    query, last_key, first_key, key_diag, value_diag, column, order, result, scores, peaks,
):
    tokens = q_ref.shape[0]
    blocks = W1 // tokens + 1
    pairs = q_ref.shape[1] // (2 * HD)
    lines = query.shape[1]
    rows = lines * W2
    rate = HD ** -0.5 * math.log2(math.e)
    slab = place[0]
    start = pl.multiple_of(place[1] * tokens, tokens)

    def twice(x):
        return jnp.concatenate([x, x], axis=-1)

    def diag(x):
        zero = jnp.zeros_like(x)
        return jnp.concatenate(
            [jnp.concatenate([x, zero], axis=1), jnp.concatenate([zero, x], axis=1)], axis=0
        )

    if lines > pairs:
        query[...] = jnp.zeros(query.shape, query.dtype)
    for pair in range(pairs):
        query[:, pair, :] = q_ref[:, pair * 2 * HD:(pair + 1) * 2 * HD].astype(jnp.float32)
    for j in range(blocks):
        there = pl.ds(start + j * tokens, tokens)
        key = k1_ref[there, :].T
        if j < blocks - 1:
            value_diag[j] = diag(v1_ref[there, :])
        if j == 0:
            first_key[...] = key
        elif j == blocks - 1:
            last_key[...] = key
        else:
            key_diag[j - 1] = diag(key)
    order[...] = lax.broadcasted_iota(jnp.int32, order.shape, 0).astype(jnp.float32).astype(order.dtype)
    column[...] = lax.broadcasted_iota(jnp.int32, column.shape, 1).astype(jnp.float32).astype(column.dtype)

    def used(behind):
        return [0] + list(range(blocks - 1 - behind, blocks - 1))[-(blocks - 2):] if behind else [0]

    def score(position, slot, behind):
        line = query[position]
        line = jnp.concatenate([line] * (16 // lines), axis=0).astype(jnp.bfloat16)
        mixed = []
        for start in range(0, W2, 16 // lines):
            near = [
                jnp.broadcast_to(k2_ref[pl.ds(position + 1 + start + step, 1), :], (lines, HD))
                for step in range(16 // lines)
            ]
            mixed.append(line * twice(jnp.concatenate(near, axis=0).astype(jnp.bfloat16)))
        mixed = jnp.concatenate(mixed, axis=0)
        here = jnp.broadcast_to(position, (16, tokens)).astype(jnp.float32).astype(jnp.bfloat16)
        late = jnp.concatenate([column[...] <= here] * (HD // 16), axis=0)
        if behind < blocks - 1:
            bias = lax.broadcasted_iota(jnp.int32, (1, 2 * tokens), 1) % tokens <= position
            bias = jnp.where(bias, 0.0, -jnp.inf)[None]
            if behind * tokens < W2 - 1:
                shown = lax.broadcasted_iota(jnp.int32, (W2, 1, 1), 0) + (position + behind * tokens)
                bias = bias + jnp.where(shown >= W2 - 1, 0.0, -jnp.inf)
        peak = None
        for j in used(behind):
            if j == 0:
                weights = diag(jnp.where(late, last_key[...], first_key[...]))
            else:
                weights = key_diag[j - 1]
            part = jnp.dot(mixed, weights, preferred_element_type=jnp.float32)
            if j == 0 and behind < blocks - 1:
                part = (part.reshape(W2, lines, 2 * tokens) + bias).reshape(part.shape)
            scores[slot, j] = part
            high = jnp.max(part.reshape(W2, lines, 2 * tokens), axis=0)
            peak = high if peak is None else jnp.maximum(peak, high)
        left = jnp.max(peak[:, :tokens], axis=1, keepdims=True) * rate
        right = jnp.max(peak[:, tokens:], axis=1, keepdims=True) * rate
        peaks[slot] = jnp.concatenate(
            [jnp.broadcast_to(left, (lines, tokens)), jnp.broadcast_to(right, (lines, tokens))], axis=1
        )

    def blend(position, slot, behind):
        base = pl.multiple_of(position // 16 * 16, 16)
        close = pl.multiple_of(start + base, 16)
        far = pl.multiple_of(start + (blocks - 1) * tokens + base, 16)
        late = order[...] <= jnp.broadcast_to(position - base, (16, HD)).astype(jnp.float32).astype(jnp.bfloat16)
        value = jnp.where(late, v1_ref[pl.ds(far, 16), :], v1_ref[pl.ds(close, 16), :])
        value_diag[0, pl.ds(base, 16), :HD] = value
        value_diag[0, pl.ds(pl.multiple_of(tokens + base, 16), 16), HD:] = value
        peak = peaks[slot][None]
        blended = total = None
        for j in used(behind):
            part = scores[slot, j].reshape(W2, lines, 2 * tokens)
            part = jnp.exp2(part * rate - peak)
            add = jnp.sum(part, axis=0)
            total = add if total is None else total + add
            part = jnp.dot(
                part.reshape(rows, 2 * tokens).astype(jnp.bfloat16), value_diag[j],
                preferred_element_type=jnp.float32,
            )
            blended = part if blended is None else blended + part
        acc = None
        for step in range(W2):
            near = jnp.broadcast_to(v2_ref[pl.ds(position + 1 + step, 1), :], (lines, HD))
            part = twice(near) * blended[step * lines:(step + 1) * lines]
            acc = part if acc is None else acc + part
        left = jnp.sum(total[:, :tokens], axis=1, keepdims=True)
        right = jnp.sum(total[:, tokens:], axis=1, keepdims=True)
        result[position] = jnp.concatenate([acc[:, :HD] / left, acc[:, HD:] / right], axis=1)

    def run(behind):
        for step in range(GROUP):
            score(step, step, behind)

        def trip(index, _):
            for half in range(2):
                first = (2 * index + half) * GROUP
                for step in range(GROUP):
                    ahead = jnp.minimum(first + GROUP + step, tokens - 1)
                    score(ahead, (1 - half) * GROUP + step, behind)
                    blend(first + step, half * GROUP + step, behind)
            return 0

        lax.fori_loop(0, tokens // (2 * GROUP), trip, 0)

    for behind in range(blocks):
        pl.when(jnp.minimum(slab, blocks - 1) == behind)(functools.partial(run, behind))

    for pair in range(pairs):
        out_ref[:, pair * 2 * HD:(pair + 1) * 2 * HD] = result[:, pair, :].astype(out_ref.dtype)


def attention_of(place, queries, key_one, value_one, key_two, value_two):
    tokens, width = queries.shape
    blocks = W1 // tokens + 1
    pairs = width // (2 * HD)
    lines = -(-pairs // 8) * 8
    rows = lines * W2
    vmem = pl.BlockSpec(memory_space=pltpu.VMEM)
    return pl.pallas_call(
        attention_kernel,
        out_shape=jax.ShapeDtypeStruct((tokens, width), jnp.bfloat16),
        in_specs=[pl.BlockSpec(memory_space=pltpu.SMEM)] + [vmem] * 5,
        out_specs=vmem,
        scratch_shapes=[
            pltpu.VMEM((tokens, lines, 2 * HD), jnp.float32),
            pltpu.VMEM((HD, tokens), jnp.bfloat16),
            pltpu.VMEM((HD, tokens), jnp.bfloat16),
            pltpu.VMEM((blocks - 2, 2 * HD, 2 * tokens), jnp.bfloat16),
            pltpu.VMEM((blocks - 1, 2 * tokens, 2 * HD), jnp.bfloat16),
            pltpu.VMEM((16, tokens), jnp.bfloat16),
            pltpu.VMEM((16, HD), jnp.bfloat16),
            pltpu.VMEM((tokens, lines, 2 * HD), jnp.float32),
            pltpu.VMEM((2 * GROUP, blocks - 1, rows, 2 * tokens), jnp.float32),
            pltpu.VMEM((2 * GROUP, lines, 2 * tokens), jnp.float32),
        ],
        compiler_params=pltpu.CompilerParams(vmem_limit_bytes=48 * 1024 * 1024),
        name="attention",
    )(
        place,
        queries,
        key_one,
        value_one,
        key_two.astype(jnp.float32),
        value_two.astype(jnp.float32),
    )


def body(hidden_in, query_weight, shared_weight, out_weight, residual, norm_gain):
    local_part = jnp.dot(hidden_in, shared_weight, preferred_element_type=jnp.float32).astype(
        jnp.bfloat16
    )
    width = query_weight.shape[1] // PIECES

    def project(piece, source):
        weight = query_weight[:, piece * width : (piece + 1) * width]
        return jnp.dot(source, weight, preferred_element_type=jnp.float32).astype(jnp.bfloat16)

    window, start, queries = window_of(
        local_part, hidden_in, [functools.partial(project, piece) for piece in range(PIECES)]
    )
    queries = jnp.concatenate(queries, axis=1)
    place = jnp.stack([lax.axis_index("ctx"), start]).astype(jnp.int32)
    attention = attention_of(place, queries, *window)
    summed = sum_to_owner(
        jnp.dot(attention, out_weight, preferred_element_type=jnp.float32), "head"
    )
    residual_out = (residual.astype(jnp.float32) + summed).astype(jnp.bfloat16)
    values = residual_out.astype(jnp.float32)
    scale = lax.rsqrt(jnp.mean(values * values, axis=1, keepdims=True) + 1e-05)
    normed_local = (values * scale * norm_gain).astype(jnp.bfloat16)
    normed = share_rows(normed_local, "head")
    return (residual_out, normed)


def solution(mesh):
    in_specs = (
        P("ctx", None),
        P(None, "head"),
        P(None, "head"),
        P("head", None),
        P(("ctx", "head"), None),
        P(),
    )
    out_specs = (P(("ctx", "head"), None), P("ctx", None))
    return jax.shard_map(body, mesh=mesh, in_specs=in_specs, out_specs=out_specs, check_vma=False)
```

```python
import functools
import math

import jax
import jax.numpy as jnp
from jax import lax
from jax.experimental import pallas as pl
from jax.experimental.pallas import tpu as pltpu
from jax.sharding import PartitionSpec as P

HD = 128
W1 = 512
W2 = 32
GROUP = 2
PIECES = 8


def from_behind(value, axis, steps):
    count = lax.axis_size(axis)
    initial, last = (max(0, -steps), min(count, count - steps))
    return lax.ppermute(value, axis, [(source, source + steps) for source in range(initial, last)])


def swap(value, axis, bit):
    count = lax.axis_size(axis)
    return lax.ppermute(value, axis, [(source, source ^ (1 << bit)) for source in range(count)])


def pick(value, place, dim):
    return lax.dynamic_index_in_dim(value, place, dim, keepdims=False)


def sum_to_owner(kept, sent, axis):
    count = lax.axis_size(axis)
    place = lax.axis_index(axis)
    value = kept + swap(sent, axis, 0).astype(jnp.float32)
    value = value.reshape(count // 2, -1, value.shape[1])
    for bit in range(1, count.bit_length() - 1):
        value = value.reshape(value.shape[0] // 2, 2, *value.shape[1:])
        mine = (place >> bit) & 1
        value = pick(value, mine, 1) + swap(
            pick(value, 1 - mine, 1).astype(jnp.bfloat16), axis, bit
        ).astype(jnp.float32)
    return value[0]


def share_rows(value, axis):
    count = lax.axis_size(axis)
    place = lax.axis_index(axis)
    rows, width = value.shape
    value = value[None]
    for bit in reversed(range(count.bit_length() - 1)):
        mine = (place >> bit) & 1
        other = swap(value, axis, bit)
        value = jnp.where(mine == 0, jnp.stack([value, other], 1), jnp.stack([other, value], 1))
        value = value.reshape(-1, rows, width)
    return value.reshape(-1, width)


def gather_columns(value):
    count = value.shape[0] * value.shape[1]
    return value.reshape(count, *value.shape[2:]).transpose(1, 0, 2).reshape(value.shape[2], -1)


def simple_window(local_part):
    tokens = local_part.shape[0]
    shared = lax.all_gather(local_part, "head", axis=1, tiled=True)
    first_pair = shared[:, : 2 * HD]
    second_pair = shared[:, 2 * HD :]
    reach = W1 // tokens
    earlier, rim = from_behind((first_pair, second_pair[tokens - W2 :]), "ctx", 1)
    pieces = [earlier]
    for distance in range(2, reach + 1):
        pieces.append(from_behind(first_pair, "ctx", distance))
    one = jnp.concatenate(pieces[::-1] + [first_pair], 0)
    two = jnp.concatenate([rim, second_pair], 0)
    return one[:, :HD], one[:, HD:], two[:, :HD], two[:, HD:]


def window_of(local_part, source, work):
    done = []

    def beside(values):
        nonlocal source
        if done:
            values, source, done[-1] = lax.optimization_barrier((values, source, done[-1]))
        done.append(work[len(done)](source))
        return values

    tokens = local_part.shape[0]
    heads = lax.axis_size("head")
    odd = lax.axis_index("ctx") & 1
    place = lax.axis_index("head")
    if heads < 4 or lax.axis_size("ctx") % 2 or W1 != 4 * tokens:
        return simple_window(local_part), [piece(source) for piece in work]
    value = beside(local_part[None])
    for bit in reversed(range(1, heads.bit_length() - 1)):
        other = swap(value, "head", bit)
        mine = (place >> bit) & 1
        value = jnp.stack([jnp.where(mine == 0, value, other), jnp.where(mine == 0, other, value)], 1)
        value = value.reshape(-1, *local_part.shape)
    half = value.shape[0] // 2
    first, second = value[:half], value[half:]
    rim = second[:, tokens - W2 :]
    first_rim, first = beside((jnp.concatenate([first, rim], 1), first))
    two_back = from_behind(first_rim, "ctx", 2)
    four_back = from_behind(first, "ctx", 4)
    two_back, two_rim = two_back[:, :tokens], two_back[:, tokens:]
    sent = jnp.concatenate([four_back, two_back, first, jnp.where(odd == 0, rim, two_rim)], 1)
    other = swap(beside(sent), "ctx", 0)
    far, near, there = (other[:, step * tokens : (step + 1) * tokens] for step in range(3))
    value = jnp.concatenate(
        [
            four_back,
            jnp.where(odd == 0, far, near),
            two_back,
            jnp.where(odd == 0, near, there),
            first,
            other[:, 3 * tokens :],
            second,
        ],
        1,
    )
    other = swap(value, "head", 0)
    mine = place & 1
    value = jnp.stack([jnp.where(mine == 0, value, other), jnp.where(mine == 0, other, value)], 1)
    one, two = value[:, :, : W1 + tokens], value[:, :, W1 + tokens :]
    one, two = gather_columns(one), gather_columns(two)
    return (one[:, :HD], one[:, HD:], two[:, :HD], two[:, HD:]), done


def attention_kernel(
    place, q_first, q_middle, q_last, k1_ref, v1_ref, k2_ref, v2_ref, weight_hbm, kept_ref, sent_ref,
    weight, arrived, attention, query, last_key, first_key, key_diag, value_diag, column, order, result, scores, peaks,
    *, count,
):
    tokens = q_first.shape[0]
    share = tokens // count
    blocks = W1 // tokens + 1
    width = q_first.shape[1] + q_middle.shape[1] + q_last.shape[1]
    pairs = width // (2 * HD)
    lines = query.shape[1]
    rows = lines * W2
    rate = HD ** -0.5 * math.log2(math.e)
    slab = place[0]
    side = place[1]

    def twice(x):
        return jnp.concatenate([x, x], axis=-1)

    def diag(x):
        zero = jnp.zeros_like(x)
        return jnp.concatenate(
            [jnp.concatenate([x, zero], axis=1), jnp.concatenate([zero, x], axis=1)], axis=0
        )

    copies = [
        pltpu.make_async_copy(
            weight_hbm.at[pair * 2 * HD:(pair + 1) * 2 * HD], weight.at[pair * 2 * HD:(pair + 1) * 2 * HD],
            arrived.at[pair],
        )
        for pair in range(pairs)
    ]
    for copy in copies:
        copy.start()
    if lines > pairs:
        query[...] = jnp.zeros(query.shape, query.dtype)
    line = 0
    for part in (q_first, q_middle, q_last):
        for lane in range(0, part.shape[1], HD):
            half = line % 2 * HD
            query[:, line // 2, half:half + HD] = part[:, lane:lane + HD].astype(jnp.float32)
            line += 1
    for j in range(blocks):
        there = slice(j * tokens, (j + 1) * tokens)
        key = k1_ref[there, :].T
        if j < blocks - 1:
            value_diag[j] = diag(v1_ref[there, :])
        if j == 0:
            first_key[...] = key
        elif j == blocks - 1:
            last_key[...] = key
        else:
            key_diag[j - 1] = diag(key)
    order[...] = lax.broadcasted_iota(jnp.int32, order.shape, 0).astype(jnp.float32).astype(order.dtype)
    column[...] = lax.broadcasted_iota(jnp.int32, column.shape, 1).astype(jnp.float32).astype(column.dtype)

    def used(behind):
        return [0] + list(range(blocks - 1 - behind, blocks - 1))[-(blocks - 2):] if behind else [0]

    def score(position, slot, behind):
        line = query[position]
        line = jnp.concatenate([line] * (16 // lines), axis=0).astype(jnp.bfloat16)
        mixed = []
        for start in range(0, W2, 16 // lines):
            near = [
                jnp.broadcast_to(k2_ref[pl.ds(position + 1 + start + step, 1), :], (lines, HD))
                for step in range(16 // lines)
            ]
            mixed.append(line * twice(jnp.concatenate(near, axis=0).astype(jnp.bfloat16)))
        mixed = jnp.concatenate(mixed, axis=0)
        here = jnp.broadcast_to(position, (16, tokens)).astype(jnp.float32).astype(jnp.bfloat16)
        late = jnp.concatenate([column[...] <= here] * (HD // 16), axis=0)
        if behind < blocks - 1:
            bias = lax.broadcasted_iota(jnp.int32, (1, 2 * tokens), 1) % tokens <= position
            bias = jnp.where(bias, 0.0, -jnp.inf)[None]
            if behind * tokens < W2 - 1:
                shown = lax.broadcasted_iota(jnp.int32, (W2, 1, 1), 0) + (position + behind * tokens)
                bias = bias + jnp.where(shown >= W2 - 1, 0.0, -jnp.inf)
        peak = None
        for j in used(behind):
            if j == 0:
                weights = diag(jnp.where(late, last_key[...], first_key[...]))
            else:
                weights = key_diag[j - 1]
            part = jnp.dot(mixed, weights, preferred_element_type=jnp.float32)
            if j == 0 and behind < blocks - 1:
                part = (part.reshape(W2, lines, 2 * tokens) + bias).reshape(part.shape)
            scores[slot, j] = part
            high = jnp.max(part.reshape(W2, lines, 2 * tokens), axis=0)
            peak = high if peak is None else jnp.maximum(peak, high)
        left = jnp.max(peak[:, :tokens], axis=1, keepdims=True) * rate
        right = jnp.max(peak[:, tokens:], axis=1, keepdims=True) * rate
        peaks[slot] = jnp.concatenate(
            [jnp.broadcast_to(left, (lines, tokens)), jnp.broadcast_to(right, (lines, tokens))], axis=1
        )

    def blend(position, slot, behind):
        base = pl.multiple_of(position // 16 * 16, 16)
        far = pl.multiple_of((blocks - 1) * tokens + base, 16)
        late = order[...] <= jnp.broadcast_to(position - base, (16, HD)).astype(jnp.float32).astype(jnp.bfloat16)
        value = jnp.where(late, v1_ref[pl.ds(far, 16), :], v1_ref[pl.ds(base, 16), :])
        value_diag[0, pl.ds(base, 16), :HD] = value
        value_diag[0, pl.ds(pl.multiple_of(tokens + base, 16), 16), HD:] = value
        peak = peaks[slot][None]
        blended = total = None
        for j in used(behind):
            part = scores[slot, j].reshape(W2, lines, 2 * tokens)
            part = jnp.exp2(part * rate - peak)
            add = jnp.sum(part, axis=0)
            total = add if total is None else total + add
            part = jnp.dot(
                part.reshape(rows, 2 * tokens).astype(jnp.bfloat16), value_diag[j],
                preferred_element_type=jnp.float32,
            )
            blended = part if blended is None else blended + part
        acc = None
        for step in range(W2):
            near = jnp.broadcast_to(v2_ref[pl.ds(position + 1 + step, 1), :], (lines, HD))
            part = twice(near) * blended[step * lines:(step + 1) * lines]
            acc = part if acc is None else acc + part
        left = jnp.sum(total[:, :tokens], axis=1, keepdims=True)
        right = jnp.sum(total[:, tokens:], axis=1, keepdims=True)
        result[position] = jnp.concatenate([acc[:, :HD] / left, acc[:, HD:] / right], axis=1)

    def run(behind):
        for step in range(GROUP):
            score(step, step, behind)

        def trip(index, _):
            for half in range(2):
                first = (2 * index + half) * GROUP
                for step in range(GROUP):
                    ahead = jnp.minimum(first + GROUP + step, tokens - 1)
                    score(ahead, (1 - half) * GROUP + step, behind)
                    blend(first + step, half * GROUP + step, behind)
            return 0

        lax.fori_loop(0, tokens // (2 * GROUP), trip, 0)

    for behind in range(blocks):
        pl.when(jnp.minimum(slab, blocks - 1) == behind)(functools.partial(run, behind))

    for pair in range(pairs):
        attention[:, pair * 2 * HD:(pair + 1) * 2 * HD] = result[:, pair, :].astype(attention.dtype)
    for copy in copies:
        copy.wait()
    step = min(1024, weight.shape[1])
    for lane in range(0, weight.shape[1], step):
        product = jnp.dot(
            attention[...], weight[:, lane:lane + step], preferred_element_type=jnp.float32
        ).reshape(-1, 2, share, step)
        even, odd = product[:, 0], product[:, 1]
        kept = jnp.where(side == 0, even, odd)
        sent = jnp.where(side == 0, odd, even)
        kept_ref[:, lane:lane + step] = kept.reshape(-1, step)
        sent_ref[:, lane:lane + step] = sent.reshape(-1, step).astype(sent_ref.dtype)


def project_kernel(source, weight_hbm, out, weight, arrived, *, lane):
    width = out.shape[1]
    size = weight.shape[0] // PIECES
    rows = [slice(step * size, (step + 1) * size) for step in range(PIECES)]
    copies = [
        pltpu.make_async_copy(weight_hbm.at[part, lane:lane + width], weight.at[part], arrived.at[step])
        for step, part in enumerate(rows)
    ]
    for copy in copies:
        copy.start()
    product = None
    for copy, part in zip(copies, rows):
        copy.wait()
        add = jnp.dot(source[:, part], weight[part, :], preferred_element_type=jnp.float32)
        product = add if product is None else product + add
    out[...] = product.astype(out.dtype)


def project(weight, lane, width, source):
    vmem = pl.BlockSpec(memory_space=pltpu.VMEM)
    return pl.pallas_call(
        functools.partial(project_kernel, lane=lane),
        out_shape=jax.ShapeDtypeStruct((source.shape[0], width), jnp.bfloat16),
        in_specs=[vmem, pl.BlockSpec(memory_space=pl.ANY)],
        out_specs=vmem,
        scratch_shapes=[
            pltpu.VMEM((weight.shape[0], width), weight.dtype), pltpu.SemaphoreType.DMA((PIECES,)),
        ],
        compiler_params=pltpu.CompilerParams(vmem_limit_bytes=16 * 1024 * 1024),
        cost_estimate=pl.CostEstimate(
            flops=2 * source.shape[0] * weight.shape[0] * width,
            bytes_accessed=2 * weight.shape[0] * width,
            transcendentals=0,
        ),
        name="project",
    )(source, weight)


def attention_of(place, count, queries, key_one, value_one, key_two, value_two, out_weight):
    tokens = queries[0].shape[0]
    width = out_weight.shape[0]
    blocks = W1 // tokens + 1
    pairs = width // (2 * HD)
    lines = -(-pairs // 8) * 8
    rows = lines * W2
    vmem = pl.BlockSpec(memory_space=pltpu.VMEM)
    return pl.pallas_call(
        functools.partial(attention_kernel, count=count),
        out_shape=(
            jax.ShapeDtypeStruct((tokens // 2, out_weight.shape[1]), jnp.float32),
            jax.ShapeDtypeStruct((tokens // 2, out_weight.shape[1]), jnp.bfloat16),
        ),
        in_specs=[pl.BlockSpec(memory_space=pltpu.SMEM)] + [vmem] * 7 + [pl.BlockSpec(memory_space=pl.ANY)],
        out_specs=(vmem, vmem),
        scratch_shapes=[
            pltpu.VMEM(out_weight.shape, out_weight.dtype),
            pltpu.SemaphoreType.DMA((pairs,)),
            pltpu.VMEM((tokens, width), jnp.bfloat16),
            pltpu.VMEM((tokens, lines, 2 * HD), jnp.float32),
            pltpu.VMEM((HD, tokens), jnp.bfloat16),
            pltpu.VMEM((HD, tokens), jnp.bfloat16),
            pltpu.VMEM((blocks - 2, 2 * HD, 2 * tokens), jnp.bfloat16),
            pltpu.VMEM((blocks - 1, 2 * tokens, 2 * HD), jnp.bfloat16),
            pltpu.VMEM((16, tokens), jnp.bfloat16),
            pltpu.VMEM((16, HD), jnp.bfloat16),
            pltpu.VMEM((tokens, lines, 2 * HD), jnp.float32),
            pltpu.VMEM((2 * GROUP, blocks - 1, rows, 2 * tokens), jnp.float32),
            pltpu.VMEM((2 * GROUP, lines, 2 * tokens), jnp.float32),
        ],
        compiler_params=pltpu.CompilerParams(vmem_limit_bytes=40 * 1024 * 1024),
        name="attention",
    )(
        place,
        *queries,
        key_one,
        value_one,
        key_two.astype(jnp.float32),
        value_two.astype(jnp.float32),
        out_weight,
    )


def body(hidden_in, query_weight, shared_weight, out_weight, residual, norm_gain):
    local_part = jnp.dot(hidden_in, shared_weight, preferred_element_type=jnp.float32).astype(
        jnp.bfloat16
    )
    half = query_weight.shape[1] // 2
    query_weight = pltpu.with_memory_space_constraint(query_weight, pltpu.HBM)
    window, queries = window_of(
        local_part,
        hidden_in,
        [
            functools.partial(project, query_weight, lane, width)
            for lane, width in ((0, half // 2), (half // 2, half), (half // 2 + half, half // 2))
        ],
    )
    place = jnp.stack([lax.axis_index("ctx"), lax.axis_index("head") & 1]).astype(jnp.int32)
    kept, sent = attention_of(place, lax.axis_size("head"), queries, *window, out_weight)
    summed = sum_to_owner(kept, sent, "head")
    residual_out = (residual.astype(jnp.float32) + summed).astype(jnp.bfloat16)
    values = residual_out.astype(jnp.float32)
    scale = lax.rsqrt(jnp.mean(values * values, axis=1, keepdims=True) + 1e-05)
    normed_local = (values * scale * norm_gain).astype(jnp.bfloat16)
    normed = share_rows(normed_local, "head")
    return (residual_out, normed)


def solution(mesh):
    in_specs = (
        P("ctx", None),
        P(None, "head"),
        P(None, "head"),
        P("head", None),
        P(("ctx", "head"), None),
        P(),
    )
    out_specs = (P(("ctx", "head"), None), P("ctx", None))
    return jax.shard_map(body, mesh=mesh, in_specs=in_specs, out_specs=out_specs, check_vma=False)
```

```python
import functools
import math

import jax
import jax.numpy as jnp
from jax import lax
from jax.experimental import pallas as pl
from jax.experimental.pallas import tpu as pltpu
from jax.sharding import PartitionSpec as P

HD = 128
W1 = 512
W2 = 32
GROUP = 2
PIECES = 4


def from_behind(value, axis, steps):
    count = lax.axis_size(axis)
    initial, last = (max(0, -steps), min(count, count - steps))
    return lax.ppermute(value, axis, [(source, source + steps) for source in range(initial, last)])


def swap(value, axis, bit):
    count = lax.axis_size(axis)
    return lax.ppermute(value, axis, [(source, source ^ (1 << bit)) for source in range(count)])


def pick(value, place, dim):
    return lax.dynamic_index_in_dim(value, place, dim, keepdims=False)


def sum_to_owner(kept, sent, axis):
    count = lax.axis_size(axis)
    place = lax.axis_index(axis)
    value = kept + swap(sent, axis, 0).astype(jnp.float32)
    value = value.reshape(count // 2, -1, value.shape[1])
    for bit in range(1, count.bit_length() - 1):
        value = value.reshape(value.shape[0] // 2, 2, *value.shape[1:])
        mine = (place >> bit) & 1
        value = pick(value, mine, 1) + swap(
            pick(value, 1 - mine, 1).astype(jnp.bfloat16), axis, bit
        ).astype(jnp.float32)
    return value[0]


def share_rows(value, axis):
    count = lax.axis_size(axis)
    place = lax.axis_index(axis)
    rows, width = value.shape
    value = value[None]
    for bit in reversed(range(count.bit_length() - 1)):
        mine = (place >> bit) & 1
        other = swap(value, axis, bit)
        value = jnp.where(mine == 0, jnp.stack([value, other], 1), jnp.stack([other, value], 1))
        value = value.reshape(-1, rows, width)
    return value.reshape(-1, width)


def gather_columns(value):
    count = value.shape[0] * value.shape[1]
    return value.reshape(count, *value.shape[2:]).transpose(1, 0, 2).reshape(value.shape[2], -1)


def simple_window(local_part):
    tokens = local_part.shape[0]
    shared = lax.all_gather(local_part, "head", axis=1, tiled=True)
    first_pair = shared[:, : 2 * HD]
    second_pair = shared[:, 2 * HD :]
    reach = W1 // tokens
    earlier, rim = from_behind((first_pair, second_pair[tokens - W2 :]), "ctx", 1)
    pieces = [earlier]
    for distance in range(2, reach + 1):
        pieces.append(from_behind(first_pair, "ctx", distance))
    one = jnp.concatenate(pieces[::-1] + [first_pair], 0)
    two = jnp.concatenate([rim, second_pair], 0)
    return one[:, :HD], one[:, HD:], two[:, :HD], two[:, HD:]


def window_of(local_part, source, work):
    done = []

    def beside(values):
        nonlocal source
        if done:
            values, source, done[-1] = lax.optimization_barrier((values, source, done[-1]))
        done.append(work[len(done)](source))
        return values

    tokens = local_part.shape[0]
    heads = lax.axis_size("head")
    odd = lax.axis_index("ctx") & 1
    place = lax.axis_index("head")
    if heads < 4 or lax.axis_size("ctx") % 2 or W1 != 4 * tokens:
        return simple_window(local_part), [piece(source) for piece in work]
    value = beside(local_part[None])
    for bit in reversed(range(1, heads.bit_length() - 1)):
        other = swap(value, "head", bit)
        mine = (place >> bit) & 1
        value = jnp.stack([jnp.where(mine == 0, value, other), jnp.where(mine == 0, other, value)], 1)
        value = value.reshape(-1, *local_part.shape)
    half = value.shape[0] // 2
    first, second = value[:half], value[half:]
    rim = second[:, tokens - W2 :]
    first_rim, first = beside((jnp.concatenate([first, rim], 1), first))
    two_back = from_behind(first_rim, "ctx", 2)
    four_back = from_behind(first, "ctx", 4)
    two_back, two_rim = two_back[:, :tokens], two_back[:, tokens:]
    sent = jnp.concatenate([four_back, two_back, first, jnp.where(odd == 0, rim, two_rim)], 1)
    other = swap(beside(sent), "ctx", 0)
    other, done[-1] = lax.optimization_barrier((other, done[-1]))
    far, near, there = (other[:, step * tokens : (step + 1) * tokens] for step in range(3))
    value = jnp.concatenate(
        [
            four_back,
            jnp.where(odd == 0, far, near),
            two_back,
            jnp.where(odd == 0, near, there),
            first,
            other[:, 3 * tokens :],
            second,
        ],
        1,
    )
    other = swap(value, "head", 0)
    mine = place & 1
    value = jnp.stack([jnp.where(mine == 0, value, other), jnp.where(mine == 0, other, value)], 1)
    one, two = value[:, :, : W1 + tokens], value[:, :, W1 + tokens :]
    one, two = gather_columns(one), gather_columns(two)
    return (one[:, :HD], one[:, HD:], two[:, :HD], two[:, HD:]), done


def attention_kernel(
    place, q_first, q_middle, q_last, k1_ref, v1_ref, k2_ref, v2_ref, weight_hbm, kept_ref, sent_ref,
    weight, arrived, attention, query, last_key, first_key, key_diag, value_diag, column, order, result, scores, peaks,
    *, count,
):
    tokens = q_first.shape[0]
    share = tokens // count
    blocks = W1 // tokens + 1
    width = q_first.shape[1] + q_middle.shape[1] + q_last.shape[1]
    pairs = width // (2 * HD)
    lines = query.shape[1]
    rows = lines * W2
    rate = HD ** -0.5 * math.log2(math.e)
    slab = place[0]
    side = place[1]

    def twice(x):
        return jnp.concatenate([x, x], axis=-1)

    def diag(x):
        zero = jnp.zeros_like(x)
        return jnp.concatenate(
            [jnp.concatenate([x, zero], axis=1), jnp.concatenate([zero, x], axis=1)], axis=0
        )

    copies = [
        pltpu.make_async_copy(
            weight_hbm.at[pair * 2 * HD:(pair + 1) * 2 * HD], weight.at[pair * 2 * HD:(pair + 1) * 2 * HD],
            arrived.at[pair],
        )
        for pair in range(pairs)
    ]
    for copy in copies:
        copy.start()
    if lines > pairs:
        query[...] = jnp.zeros(query.shape, query.dtype)
    line = 0
    for part in (q_first, q_middle, q_last):
        for lane in range(0, part.shape[1], HD):
            half = line % 2 * HD
            query[:, line // 2, half:half + HD] = part[:, lane:lane + HD].astype(jnp.float32)
            line += 1
    for j in range(blocks):
        there = slice(j * tokens, (j + 1) * tokens)
        key = k1_ref[there, :].T
        if j < blocks - 1:
            value_diag[j] = diag(v1_ref[there, :])
        if j == 0:
            first_key[...] = key
        elif j == blocks - 1:
            last_key[...] = key
        else:
            key_diag[j - 1] = diag(key)
    order[...] = lax.broadcasted_iota(jnp.int32, order.shape, 0).astype(jnp.float32).astype(order.dtype)
    column[...] = lax.broadcasted_iota(jnp.int32, column.shape, 1).astype(jnp.float32).astype(column.dtype)

    def used(behind):
        return [0] + list(range(blocks - 1 - behind, blocks - 1))[-(blocks - 2):] if behind else [0]

    def score(position, slot, behind):
        line = query[position]
        line = jnp.concatenate([line] * (16 // lines), axis=0).astype(jnp.bfloat16)
        mixed = []
        for start in range(0, W2, 16 // lines):
            near = [
                jnp.broadcast_to(k2_ref[pl.ds(position + 1 + start + step, 1), :], (lines, HD))
                for step in range(16 // lines)
            ]
            mixed.append(line * twice(jnp.concatenate(near, axis=0).astype(jnp.bfloat16)))
        mixed = jnp.concatenate(mixed, axis=0)
        here = jnp.broadcast_to(position, (16, tokens)).astype(jnp.float32).astype(jnp.bfloat16)
        late = jnp.concatenate([column[...] <= here] * (HD // 16), axis=0)
        if behind < blocks - 1:
            bias = lax.broadcasted_iota(jnp.int32, (1, 2 * tokens), 1) % tokens <= position
            bias = jnp.where(bias, 0.0, -jnp.inf)[None]
            if behind * tokens < W2 - 1:
                shown = lax.broadcasted_iota(jnp.int32, (W2, 1, 1), 0) + (position + behind * tokens)
                bias = bias + jnp.where(shown >= W2 - 1, 0.0, -jnp.inf)
        peak = None
        for j in used(behind):
            if j == 0:
                weights = diag(jnp.where(late, last_key[...], first_key[...]))
            else:
                weights = key_diag[j - 1]
            part = jnp.dot(mixed, weights, preferred_element_type=jnp.float32)
            if j == 0 and behind < blocks - 1:
                part = (part.reshape(W2, lines, 2 * tokens) + bias).reshape(part.shape)
            scores[slot, j] = part
            high = jnp.max(part.reshape(W2, lines, 2 * tokens), axis=0)
            peak = high if peak is None else jnp.maximum(peak, high)
        left = jnp.max(peak[:, :tokens], axis=1, keepdims=True) * rate
        right = jnp.max(peak[:, tokens:], axis=1, keepdims=True) * rate
        peaks[slot] = jnp.concatenate(
            [jnp.broadcast_to(left, (lines, tokens)), jnp.broadcast_to(right, (lines, tokens))], axis=1
        )

    def blend(position, slot, behind):
        base = pl.multiple_of(position // 16 * 16, 16)
        far = pl.multiple_of((blocks - 1) * tokens + base, 16)
        late = order[...] <= jnp.broadcast_to(position - base, (16, HD)).astype(jnp.float32).astype(jnp.bfloat16)
        value = jnp.where(late, v1_ref[pl.ds(far, 16), :], v1_ref[pl.ds(base, 16), :])
        value_diag[0, pl.ds(base, 16), :HD] = value
        value_diag[0, pl.ds(pl.multiple_of(tokens + base, 16), 16), HD:] = value
        peak = peaks[slot][None]
        blended = total = None
        for j in used(behind):
            part = scores[slot, j].reshape(W2, lines, 2 * tokens)
            part = jnp.exp2(part * rate - peak)
            add = jnp.sum(part, axis=0)
            total = add if total is None else total + add
            part = jnp.dot(
                part.reshape(rows, 2 * tokens).astype(jnp.bfloat16), value_diag[j],
                preferred_element_type=jnp.float32,
            )
            blended = part if blended is None else blended + part
        acc = None
        for step in range(W2):
            near = jnp.broadcast_to(v2_ref[pl.ds(position + 1 + step, 1), :], (lines, HD))
            part = twice(near) * blended[step * lines:(step + 1) * lines]
            acc = part if acc is None else acc + part
        left = jnp.sum(total[:, :tokens], axis=1, keepdims=True)
        right = jnp.sum(total[:, tokens:], axis=1, keepdims=True)
        result[position] = jnp.concatenate([acc[:, :HD] / left, acc[:, HD:] / right], axis=1)

    def run(behind):
        for step in range(GROUP):
            score(step, step, behind)

        def trip(index, _):
            for half in range(2):
                first = (2 * index + half) * GROUP
                for step in range(GROUP):
                    ahead = jnp.minimum(first + GROUP + step, tokens - 1)
                    score(ahead, (1 - half) * GROUP + step, behind)
                    blend(first + step, half * GROUP + step, behind)
            return 0

        lax.fori_loop(0, tokens // (2 * GROUP), trip, 0)

    for behind in range(blocks):
        pl.when(jnp.minimum(slab, blocks - 1) == behind)(functools.partial(run, behind))

    for pair in range(pairs):
        attention[:, pair * 2 * HD:(pair + 1) * 2 * HD] = result[:, pair, :].astype(attention.dtype)
    for copy in copies:
        copy.wait()
    step = min(1024, weight.shape[1])
    for lane in range(0, weight.shape[1], step):
        product = jnp.dot(
            attention[...], weight[:, lane:lane + step], preferred_element_type=jnp.float32
        ).reshape(-1, 2, share, step)
        even, odd = product[:, 0], product[:, 1]
        kept = jnp.where(side == 0, even, odd)
        sent = jnp.where(side == 0, odd, even)
        kept_ref[:, lane:lane + step] = kept.reshape(-1, step)
        sent_ref[:, lane:lane + step] = sent.reshape(-1, step).astype(sent_ref.dtype)


def share_kernel(source_hbm, weight_hbm, source, out, weight, arrived):
    size = weight.shape[0] // PIECES
    rows = [slice(step * size, (step + 1) * size) for step in range(PIECES)]
    copies = [
        (
            pltpu.make_async_copy(source_hbm.at[:, part], source.at[:, part], arrived.at[0, step]),
            pltpu.make_async_copy(weight_hbm.at[part], weight.at[part], arrived.at[1, step]),
        )
        for step, part in enumerate(rows)
    ]
    for one, two in copies:
        one.start()
        two.start()
    product = None
    for (one, two), part in zip(copies, rows):
        one.wait()
        two.wait()
        add = jnp.dot(source[:, part], weight[part, :], preferred_element_type=jnp.float32)
        product = add if product is None else product + add
    out[...] = product.astype(out.dtype)


def share(source, weight):
    vmem = pl.BlockSpec(memory_space=pltpu.VMEM)
    return pl.pallas_call(
        share_kernel,
        out_shape=(
            jax.ShapeDtypeStruct(source.shape, source.dtype),
            jax.ShapeDtypeStruct((source.shape[0], weight.shape[1]), jnp.bfloat16),
        ),
        in_specs=[pl.BlockSpec(memory_space=pl.ANY)] * 2,
        out_specs=(vmem, vmem),
        scratch_shapes=[pltpu.VMEM(weight.shape, weight.dtype), pltpu.SemaphoreType.DMA((2, PIECES))],
        compiler_params=pltpu.CompilerParams(vmem_limit_bytes=8 * 1024 * 1024),
        name="share",
    )(pltpu.with_memory_space_constraint(source, pltpu.HBM), pltpu.with_memory_space_constraint(weight, pltpu.HBM))


def project_kernel(source, weight_hbm, out, weight, arrived, *, lane):
    width = out.shape[1]
    size = weight.shape[0] // PIECES
    rows = [slice(step * size, (step + 1) * size) for step in range(PIECES)]
    copies = [
        pltpu.make_async_copy(weight_hbm.at[part, lane:lane + width], weight.at[part], arrived.at[step])
        for step, part in enumerate(rows)
    ]
    for copy in copies:
        copy.start()
    product = None
    for copy, part in zip(copies, rows):
        copy.wait()
        add = jnp.dot(source[:, part], weight[part, :], preferred_element_type=jnp.float32)
        product = add if product is None else product + add
    out[...] = product.astype(out.dtype)


def project(weight, lane, width, source):
    vmem = pl.BlockSpec(memory_space=pltpu.VMEM)
    return pl.pallas_call(
        functools.partial(project_kernel, lane=lane),
        out_shape=jax.ShapeDtypeStruct((source.shape[0], width), jnp.bfloat16),
        in_specs=[vmem, pl.BlockSpec(memory_space=pl.ANY)],
        out_specs=vmem,
        scratch_shapes=[
            pltpu.VMEM((weight.shape[0], width), weight.dtype), pltpu.SemaphoreType.DMA((PIECES,)),
        ],
        compiler_params=pltpu.CompilerParams(vmem_limit_bytes=16 * 1024 * 1024),
        cost_estimate=pl.CostEstimate(
            flops=2 * source.shape[0] * weight.shape[0] * width,
            bytes_accessed=2 * weight.shape[0] * width,
            transcendentals=0,
        ),
        name="project",
    )(source, weight)


def attention_of(place, count, queries, key_one, value_one, key_two, value_two, out_weight):
    tokens = queries[0].shape[0]
    width = out_weight.shape[0]
    blocks = W1 // tokens + 1
    pairs = width // (2 * HD)
    lines = -(-pairs // 8) * 8
    rows = lines * W2
    vmem = pl.BlockSpec(memory_space=pltpu.VMEM)
    return pl.pallas_call(
        functools.partial(attention_kernel, count=count),
        out_shape=(
            jax.ShapeDtypeStruct((tokens // 2, out_weight.shape[1]), jnp.float32),
            jax.ShapeDtypeStruct((tokens // 2, out_weight.shape[1]), jnp.bfloat16),
        ),
        in_specs=[pl.BlockSpec(memory_space=pltpu.SMEM)] + [vmem] * 7 + [pl.BlockSpec(memory_space=pl.ANY)],
        out_specs=(vmem, vmem),
        scratch_shapes=[
            pltpu.VMEM(out_weight.shape, out_weight.dtype),
            pltpu.SemaphoreType.DMA((pairs,)),
            pltpu.VMEM((tokens, width), jnp.bfloat16),
            pltpu.VMEM((tokens, lines, 2 * HD), jnp.float32),
            pltpu.VMEM((HD, tokens), jnp.bfloat16),
            pltpu.VMEM((HD, tokens), jnp.bfloat16),
            pltpu.VMEM((blocks - 2, 2 * HD, 2 * tokens), jnp.bfloat16),
            pltpu.VMEM((blocks - 1, 2 * tokens, 2 * HD), jnp.bfloat16),
            pltpu.VMEM((16, tokens), jnp.bfloat16),
            pltpu.VMEM((16, HD), jnp.bfloat16),
            pltpu.VMEM((tokens, lines, 2 * HD), jnp.float32),
            pltpu.VMEM((2 * GROUP, blocks - 1, rows, 2 * tokens), jnp.float32),
            pltpu.VMEM((2 * GROUP, lines, 2 * tokens), jnp.float32),
        ],
        compiler_params=pltpu.CompilerParams(vmem_limit_bytes=40 * 1024 * 1024),
        name="attention",
    )(
        place,
        *queries,
        key_one,
        value_one,
        key_two.astype(jnp.float32),
        value_two.astype(jnp.float32),
        out_weight,
    )


def body(hidden_in, query_weight, shared_weight, out_weight, residual, norm_gain):
    source, local_part = share(hidden_in, shared_weight)
    half = query_weight.shape[1] // 2
    query_weight = pltpu.with_memory_space_constraint(query_weight, pltpu.HBM)
    window, queries = window_of(
        local_part,
        source,
        [
            functools.partial(project, query_weight, lane, width)
            for lane, width in ((0, half // 2), (half // 2, half), (half // 2 + half, half // 2))
        ],
    )
    place = jnp.stack([lax.axis_index("ctx"), lax.axis_index("head") & 1]).astype(jnp.int32)
    kept, sent = attention_of(place, lax.axis_size("head"), queries, *window, out_weight)
    summed = sum_to_owner(kept, sent, "head")
    residual_out = (residual.astype(jnp.float32) + summed).astype(jnp.bfloat16)
    values = residual_out.astype(jnp.float32)
    scale = lax.rsqrt(jnp.mean(values * values, axis=1, keepdims=True) + 1e-05)
    normed_local = (values * scale * norm_gain).astype(jnp.bfloat16)
    normed = share_rows(normed_local, "head")
    return (residual_out, normed)


def solution(mesh):
    in_specs = (
        P("ctx", None),
        P(None, "head"),
        P(None, "head"),
        P("head", None),
        P(("ctx", "head"), None),
        P(),
    )
    out_specs = (P(("ctx", "head"), None), P("ctx", None))
    return jax.shard_map(body, mesh=mesh, in_specs=in_specs, out_specs=out_specs, check_vma=False)
```

```python
import functools
import math

import jax
import jax.numpy as jnp
from jax import lax
from jax.experimental import pallas as pl
from jax.experimental.pallas import tpu as pltpu
from jax.sharding import PartitionSpec as P

HD = 128
W1 = 512
W2 = 32
GROUP = 16
SHORT_GROUP = 4
HEADROOM = 60.0
FLOOR = 2.0 ** -88
PIECES = 4


def from_behind(value, axis, steps):
    count = lax.axis_size(axis)
    initial, last = (max(0, -steps), min(count, count - steps))
    return lax.ppermute(value, axis, [(source, source + steps) for source in range(initial, last)])


def swap(value, axis, bit):
    count = lax.axis_size(axis)
    return lax.ppermute(value, axis, [(source, source ^ (1 << bit)) for source in range(count)])


def pick(value, place, dim):
    return lax.dynamic_index_in_dim(value, place, dim, keepdims=False)


def sum_to_owner(kept, sent, axis):
    count = lax.axis_size(axis)
    place = lax.axis_index(axis)
    value = kept + swap(sent, axis, 0).astype(jnp.float32)
    value = value.reshape(count // 2, -1, value.shape[1])
    for bit in range(1, count.bit_length() - 1):
        value = value.reshape(value.shape[0] // 2, 2, *value.shape[1:])
        mine = (place >> bit) & 1
        value = pick(value, mine, 1) + swap(
            pick(value, 1 - mine, 1).astype(jnp.bfloat16), axis, bit
        ).astype(jnp.float32)
    return value[0]


def share_rows(value, axis):
    count = lax.axis_size(axis)
    place = lax.axis_index(axis)
    rows, width = value.shape
    value = value[None]
    for bit in reversed(range(count.bit_length() - 1)):
        mine = (place >> bit) & 1
        other = swap(value, axis, bit)
        value = jnp.where(mine == 0, jnp.stack([value, other], 1), jnp.stack([other, value], 1))
        value = value.reshape(-1, rows, width)
    return value.reshape(-1, width)


def gather_columns(value):
    count = value.shape[0] * value.shape[1]
    return value.reshape(count, *value.shape[2:]).transpose(1, 0, 2).reshape(value.shape[2], -1)


def simple_window(local_part):
    tokens = local_part.shape[0]
    shared = lax.all_gather(local_part, "head", axis=1, tiled=True)
    first_pair = shared[:, : 2 * HD]
    second_pair = shared[:, 2 * HD :]
    reach = W1 // tokens
    earlier, rim = from_behind((first_pair, second_pair[tokens - W2 :]), "ctx", 1)
    pieces = [earlier]
    for distance in range(2, reach + 1):
        pieces.append(from_behind(first_pair, "ctx", distance))
    one = jnp.concatenate(pieces[::-1] + [first_pair], 0)
    two = jnp.concatenate([rim, second_pair], 0)
    return one[:, :HD], one[:, HD:], two[:, :HD], two[:, HD:]


def window_of(local_part, source, work):
    done = []

    def beside(values):
        nonlocal source
        if done:
            values, source, done[-1] = lax.optimization_barrier((values, source, done[-1]))
        done.append(work[len(done)](source))
        return values

    tokens = local_part.shape[0]
    heads = lax.axis_size("head")
    odd = lax.axis_index("ctx") & 1
    place = lax.axis_index("head")
    if heads < 4 or lax.axis_size("ctx") % 2 or W1 != 4 * tokens:
        return simple_window(local_part), [piece(source) for piece in work]
    value = beside(local_part[None])
    for bit in reversed(range(1, heads.bit_length() - 1)):
        other = swap(value, "head", bit)
        mine = (place >> bit) & 1
        value = jnp.stack([jnp.where(mine == 0, value, other), jnp.where(mine == 0, other, value)], 1)
        value = value.reshape(-1, *local_part.shape)
    half = value.shape[0] // 2
    first, second = value[:half], value[half:]
    rim = second[:, tokens - W2 :]
    first_rim, first = beside((jnp.concatenate([first, rim], 1), first))
    two_back = from_behind(first_rim, "ctx", 2)
    four_back = from_behind(first, "ctx", 4)
    two_back, two_rim = two_back[:, :tokens], two_back[:, tokens:]
    sent = jnp.concatenate([four_back, two_back, first, jnp.where(odd == 0, rim, two_rim)], 1)
    other = swap(beside(sent), "ctx", 0)
    other, done[-1] = lax.optimization_barrier((other, done[-1]))
    far, near, there = (other[:, step * tokens : (step + 1) * tokens] for step in range(3))
    value = jnp.concatenate(
        [
            four_back,
            jnp.where(odd == 0, far, near),
            two_back,
            jnp.where(odd == 0, near, there),
            first,
            other[:, 3 * tokens :],
            second,
        ],
        1,
    )
    other = swap(value, "head", 0)
    mine = place & 1
    value = jnp.stack([jnp.where(mine == 0, value, other), jnp.where(mine == 0, other, value)], 1)
    one, two = value[:, :, : W1 + tokens], value[:, :, W1 + tokens :]
    one, two = gather_columns(one), gather_columns(two)
    return (one[:, :HD], one[:, HD:], two[:, :HD], two[:, HD:]), done


def attention_kernel(
    place, q_first, q_middle, q_last, k1_ref, v1_ref, k2_ref, v2_ref, weight_hbm, kept_ref, sent_ref,
    weight, arrived, attention, query, last_key, first_key, key_diag, value_diag, column, order, result, scores, bound,
    *, count,
):
    tokens = q_first.shape[0]
    share = tokens // count
    blocks = W1 // tokens + 1
    width = q_first.shape[1] + q_middle.shape[1] + q_last.shape[1]
    pairs = width // (2 * HD)
    lines = query.shape[1]
    rows = lines * W2
    rate = HD ** -0.5 * math.log2(math.e)
    slab = place[0]
    side = place[1]

    def twice(x):
        return jnp.concatenate([x, x], axis=-1)

    def diag(x):
        zero = jnp.zeros_like(x)
        return jnp.concatenate(
            [jnp.concatenate([x, zero], axis=1), jnp.concatenate([zero, x], axis=1)], axis=0
        )

    copies = [
        pltpu.make_async_copy(
            weight_hbm.at[pair * 2 * HD:(pair + 1) * 2 * HD], weight.at[pair * 2 * HD:(pair + 1) * 2 * HD],
            arrived.at[pair],
        )
        for pair in range(pairs)
    ]
    for copy in copies:
        copy.start()
    if lines > pairs:
        query[...] = jnp.zeros(query.shape, query.dtype)
    line = 0
    for part in (q_first, q_middle, q_last):
        for lane in range(0, part.shape[1], HD):
            half = line % 2 * HD
            query[:, line // 2, half:half + HD] = part[:, lane:lane + HD].astype(jnp.float32)
            line += 1
    for j in range(blocks):
        there = slice(j * tokens, (j + 1) * tokens)
        key = k1_ref[there, :].T
        if j < blocks - 1:
            value_diag[j] = diag(v1_ref[there, :])
        if j == 0:
            first_key[...] = key
        elif j == blocks - 1:
            last_key[...] = key
        else:
            key_diag[j - 1] = diag(key)
    order[...] = lax.broadcasted_iota(jnp.int32, order.shape, 0).astype(jnp.float32).astype(order.dtype)
    column[...] = lax.broadcasted_iota(jnp.int32, column.shape, 1).astype(jnp.float32).astype(column.dtype)

    key = k1_ref[...].astype(jnp.float32)
    longest = jnp.max(jnp.sum(key * key, axis=1, keepdims=True), axis=0, keepdims=True)
    key = k2_ref[...]
    key = (key * key).astype(jnp.bfloat16)
    row = lax.broadcasted_iota(jnp.int32, (tokens, key.shape[0]), 0)
    col = lax.broadcasted_iota(jnp.int32, (tokens, key.shape[0]), 1)
    seen = (col > row) & (col <= row + W2)
    for pair in range(lines):
        for half in (0, HD):
            line = query[:, pair, half:half + HD]
            size = lax.dot_general(
                (line * line).astype(jnp.bfloat16), key, (((1,), (1,)), ((), ())),
                preferred_element_type=jnp.float32,
            )
            size = jnp.max(jnp.where(seen, size, 0.0), axis=1, keepdims=True)
            size = jnp.sqrt(size * longest) * (1.03 * rate) - HEADROOM
            bound[:, pair, half:half + HD] = jnp.broadcast_to(size, (tokens, HD))

    def used(behind):
        return [0] + list(range(blocks - 1 - behind, blocks - 1))[-(blocks - 2):] if behind else [0]

    def products(position, behind):
        line = query[position]
        line = jnp.concatenate([line] * (16 // lines), axis=0).astype(jnp.bfloat16)
        mixed = []
        for start in range(0, W2, 16 // lines):
            near = [
                jnp.broadcast_to(k2_ref[pl.ds(position + 1 + start + step, 1), :], (lines, HD))
                for step in range(16 // lines)
            ]
            mixed.append(line * twice(jnp.concatenate(near, axis=0).astype(jnp.bfloat16)))
        mixed = jnp.concatenate(mixed, axis=0)
        here = jnp.broadcast_to(position, (16, tokens)).astype(jnp.float32).astype(jnp.bfloat16)
        late = jnp.concatenate([column[...] <= here] * (HD // 16), axis=0)
        if behind < blocks - 1:
            bias = lax.broadcasted_iota(jnp.int32, (1, 2 * tokens), 1) % tokens <= position
            bias = jnp.where(bias, 0.0, -jnp.inf)[None]
            if behind * tokens < W2 - 1:
                shown = lax.broadcasted_iota(jnp.int32, (W2, 1, 1), 0) + (position + behind * tokens)
                bias = bias + jnp.where(shown >= W2 - 1, 0.0, -jnp.inf)
        parts = []
        for j in used(behind):
            if j == 0:
                weights = diag(jnp.where(late, last_key[...], first_key[...]))
            else:
                weights = key_diag[j - 1]
            part = jnp.dot(mixed, weights, preferred_element_type=jnp.float32)
            if j == 0 and behind < blocks - 1:
                part = (part.reshape(W2, lines, 2 * tokens) + bias).reshape(part.shape)
            parts.append(part)
        return parts

    def attend(position, behind, parts, shift):
        base = pl.multiple_of(position // 16 * 16, 16)
        far = pl.multiple_of((blocks - 1) * tokens + base, 16)
        late = order[...] <= jnp.broadcast_to(position - base, (16, HD)).astype(jnp.float32).astype(jnp.bfloat16)
        value = jnp.where(late, v1_ref[pl.ds(far, 16), :], v1_ref[pl.ds(base, 16), :])
        value_diag[0, pl.ds(base, 16), :HD] = value
        value_diag[0, pl.ds(pl.multiple_of(tokens + base, 16), 16), HD:] = value
        blended = total = None
        for j, part in zip(used(behind), parts):
            part = part.reshape(W2, lines, 2 * tokens)
            part = jnp.exp2(part * rate - shift[None])
            add = jnp.sum(part, axis=0)
            total = add if total is None else total + add
            part = jnp.dot(
                part.reshape(rows, 2 * tokens).astype(jnp.bfloat16), value_diag[j],
                preferred_element_type=jnp.float32,
            )
            blended = part if blended is None else blended + part
        acc = None
        for step in range(W2):
            near = jnp.broadcast_to(v2_ref[pl.ds(position + 1 + step, 1), :], (lines, HD))
            part = twice(near) * blended[step * lines:(step + 1) * lines]
            acc = part if acc is None else acc + part
        left = jnp.sum(total[:, :tokens], axis=1, keepdims=True)
        right = jnp.sum(total[:, tokens:], axis=1, keepdims=True)
        result[position] = jnp.concatenate([acc[:, :HD] / left, acc[:, HD:] / right], axis=1)
        return jnp.broadcast_to(jnp.minimum(left, right), (lines, HD))

    def exact(behind, position, _):
        peak = None
        for j, part in zip(used(behind), products(position, behind)):
            scores[j] = part
            high = jnp.max(part.reshape(W2, lines, 2 * tokens), axis=0)
            peak = high if peak is None else jnp.maximum(peak, high)
        left = jnp.max(peak[:, :tokens], axis=1, keepdims=True) * rate
        right = jnp.max(peak[:, tokens:], axis=1, keepdims=True) * rate
        shift = jnp.concatenate(
            [jnp.broadcast_to(left, (lines, tokens)), jnp.broadcast_to(right, (lines, tokens))], axis=1
        )
        attend(position, behind, [scores[j] for j in used(behind)], shift)
        return 0

    def run(behind):
        group = GROUP if len(used(behind)) == blocks - 1 else SHORT_GROUP

        def trip(index, low):
            for step in range(group):
                position = index * group + step
                low = jnp.minimum(low, attend(position, behind, products(position, behind), bound[position]))
            return low

        low = lax.fori_loop(0, tokens // group, trip, jnp.full((lines, HD), jnp.inf, jnp.float32))
        kept_all = jnp.min(low) >= FLOOR

        @pl.when(jnp.logical_not(kept_all))
        def _():
            value_diag[0] = diag(v1_ref[:tokens, :])
            lax.fori_loop(0, tokens, functools.partial(exact, behind), 0)

    for behind in range(blocks):
        pl.when(jnp.minimum(slab, blocks - 1) == behind)(functools.partial(run, behind))

    for pair in range(pairs):
        attention[:, pair * 2 * HD:(pair + 1) * 2 * HD] = result[:, pair, :].astype(attention.dtype)
    for copy in copies:
        copy.wait()
    step = min(1024, weight.shape[1])
    for lane in range(0, weight.shape[1], step):
        product = jnp.dot(
            attention[...], weight[:, lane:lane + step], preferred_element_type=jnp.float32
        ).reshape(-1, 2, share, step)
        even, odd = product[:, 0], product[:, 1]
        kept = jnp.where(side == 0, even, odd)
        sent = jnp.where(side == 0, odd, even)
        kept_ref[:, lane:lane + step] = kept.reshape(-1, step)
        sent_ref[:, lane:lane + step] = sent.reshape(-1, step).astype(sent_ref.dtype)


def share_kernel(source_hbm, weight_hbm, source, out, weight, arrived):
    size = weight.shape[0] // PIECES
    rows = [slice(step * size, (step + 1) * size) for step in range(PIECES)]
    copies = [
        (
            pltpu.make_async_copy(source_hbm.at[:, part], source.at[:, part], arrived.at[0, step]),
            pltpu.make_async_copy(weight_hbm.at[part], weight.at[part], arrived.at[1, step]),
        )
        for step, part in enumerate(rows)
    ]
    for one, two in copies:
        one.start()
        two.start()
    product = None
    for (one, two), part in zip(copies, rows):
        one.wait()
        two.wait()
        add = jnp.dot(source[:, part], weight[part, :], preferred_element_type=jnp.float32)
        product = add if product is None else product + add
    out[...] = product.astype(out.dtype)


def share(source, weight):
    vmem = pl.BlockSpec(memory_space=pltpu.VMEM)
    return pl.pallas_call(
        share_kernel,
        out_shape=(
            jax.ShapeDtypeStruct(source.shape, source.dtype),
            jax.ShapeDtypeStruct((source.shape[0], weight.shape[1]), jnp.bfloat16),
        ),
        in_specs=[pl.BlockSpec(memory_space=pl.ANY)] * 2,
        out_specs=(vmem, vmem),
        scratch_shapes=[pltpu.VMEM(weight.shape, weight.dtype), pltpu.SemaphoreType.DMA((2, PIECES))],
        compiler_params=pltpu.CompilerParams(vmem_limit_bytes=8 * 1024 * 1024),
        name="share",
    )(pltpu.with_memory_space_constraint(source, pltpu.HBM), pltpu.with_memory_space_constraint(weight, pltpu.HBM))


def project_kernel(source, weight_hbm, out, weight, arrived, *, lane):
    width = out.shape[1]
    size = weight.shape[0] // PIECES
    rows = [slice(step * size, (step + 1) * size) for step in range(PIECES)]
    copies = [
        pltpu.make_async_copy(weight_hbm.at[part, lane:lane + width], weight.at[part], arrived.at[step])
        for step, part in enumerate(rows)
    ]
    for copy in copies:
        copy.start()
    product = None
    for copy, part in zip(copies, rows):
        copy.wait()
        add = jnp.dot(source[:, part], weight[part, :], preferred_element_type=jnp.float32)
        product = add if product is None else product + add
    out[...] = product.astype(out.dtype)


def project(weight, lane, width, source):
    vmem = pl.BlockSpec(memory_space=pltpu.VMEM)
    return pl.pallas_call(
        functools.partial(project_kernel, lane=lane),
        out_shape=jax.ShapeDtypeStruct((source.shape[0], width), jnp.bfloat16),
        in_specs=[vmem, pl.BlockSpec(memory_space=pl.ANY)],
        out_specs=vmem,
        scratch_shapes=[
            pltpu.VMEM((weight.shape[0], width), weight.dtype), pltpu.SemaphoreType.DMA((PIECES,)),
        ],
        compiler_params=pltpu.CompilerParams(vmem_limit_bytes=16 * 1024 * 1024),
        cost_estimate=pl.CostEstimate(
            flops=2 * source.shape[0] * weight.shape[0] * width,
            bytes_accessed=2 * weight.shape[0] * width,
            transcendentals=0,
        ),
        name="project",
    )(source, weight)


def attention_of(place, count, queries, key_one, value_one, key_two, value_two, out_weight):
    tokens = queries[0].shape[0]
    width = out_weight.shape[0]
    blocks = W1 // tokens + 1
    pairs = width // (2 * HD)
    lines = -(-pairs // 8) * 8
    rows = lines * W2
    vmem = pl.BlockSpec(memory_space=pltpu.VMEM)
    return pl.pallas_call(
        functools.partial(attention_kernel, count=count),
        out_shape=(
            jax.ShapeDtypeStruct((tokens // 2, out_weight.shape[1]), jnp.float32),
            jax.ShapeDtypeStruct((tokens // 2, out_weight.shape[1]), jnp.bfloat16),
        ),
        in_specs=[pl.BlockSpec(memory_space=pltpu.SMEM)] + [vmem] * 7 + [pl.BlockSpec(memory_space=pl.ANY)],
        out_specs=(vmem, vmem),
        scratch_shapes=[
            pltpu.VMEM(out_weight.shape, out_weight.dtype),
            pltpu.SemaphoreType.DMA((pairs,)),
            pltpu.VMEM((tokens, width), jnp.bfloat16),
            pltpu.VMEM((tokens, lines, 2 * HD), jnp.float32),
            pltpu.VMEM((HD, tokens), jnp.bfloat16),
            pltpu.VMEM((HD, tokens), jnp.bfloat16),
            pltpu.VMEM((blocks - 2, 2 * HD, 2 * tokens), jnp.bfloat16),
            pltpu.VMEM((blocks - 1, 2 * tokens, 2 * HD), jnp.bfloat16),
            pltpu.VMEM((16, tokens), jnp.bfloat16),
            pltpu.VMEM((16, HD), jnp.bfloat16),
            pltpu.VMEM((tokens, lines, 2 * HD), jnp.float32),
            pltpu.VMEM((blocks - 1, rows, 2 * tokens), jnp.float32),
            pltpu.VMEM((tokens, lines, 2 * HD), jnp.float32),
        ],
        compiler_params=pltpu.CompilerParams(vmem_limit_bytes=40 * 1024 * 1024),
        name="attention",
    )(
        place,
        *queries,
        key_one,
        value_one,
        key_two.astype(jnp.float32),
        value_two.astype(jnp.float32),
        out_weight,
    )


def body(hidden_in, query_weight, shared_weight, out_weight, residual, norm_gain):
    source, local_part = share(hidden_in, shared_weight)
    half = query_weight.shape[1] // 2
    query_weight = pltpu.with_memory_space_constraint(query_weight, pltpu.HBM)
    window, queries = window_of(
        local_part,
        source,
        [
            functools.partial(project, query_weight, lane, width)
            for lane, width in ((0, half // 2), (half // 2, half), (half // 2 + half, half // 2))
        ],
    )
    place = jnp.stack([lax.axis_index("ctx"), lax.axis_index("head") & 1]).astype(jnp.int32)
    kept, sent = attention_of(place, lax.axis_size("head"), queries, *window, out_weight)
    summed = sum_to_owner(kept, sent, "head")
    residual_out = (residual.astype(jnp.float32) + summed).astype(jnp.bfloat16)
    values = residual_out.astype(jnp.float32)
    scale = lax.rsqrt(jnp.mean(values * values, axis=1, keepdims=True) + 1e-05)
    normed_local = (values * scale * norm_gain).astype(jnp.bfloat16)
    normed = share_rows(normed_local, "head")
    return (residual_out, normed)


def solution(mesh):
    in_specs = (
        P("ctx", None),
        P(None, "head"),
        P(None, "head"),
        P("head", None),
        P(("ctx", "head"), None),
        P(),
    )
    out_specs = (P(("ctx", "head"), None), P("ctx", None))
    return jax.shard_map(body, mesh=mesh, in_specs=in_specs, out_specs=out_specs, check_vma=False)
```

```python
import functools
import math

import jax
import jax.numpy as jnp
from jax import lax
from jax.experimental import pallas as pl
from jax.experimental.pallas import tpu as pltpu
from jax.sharding import PartitionSpec as P

HD = 128
W1 = 512
W2 = 32
GROUP = 32
SHORT_GROUP = 4
HEADROOM = 60.0
FLOOR = 2.0 ** -88
PIECES = 4


def from_behind(value, axis, steps):
    count = lax.axis_size(axis)
    initial, last = (max(0, -steps), min(count, count - steps))
    return lax.ppermute(value, axis, [(source, source + steps) for source in range(initial, last)])


def swap(value, axis, bit):
    count = lax.axis_size(axis)
    return lax.ppermute(value, axis, [(source, source ^ (1 << bit)) for source in range(count)])


def pick(value, place, dim):
    return lax.dynamic_index_in_dim(value, place, dim, keepdims=False)


def sum_to_owner(kept, sent, axis):
    count = lax.axis_size(axis)
    place = lax.axis_index(axis)
    value = kept + swap(sent, axis, 0).astype(jnp.float32)
    value = value.reshape(count // 2, -1, value.shape[1])
    for bit in range(1, count.bit_length() - 1):
        value = value.reshape(value.shape[0] // 2, 2, *value.shape[1:])
        mine = (place >> bit) & 1
        value = pick(value, mine, 1) + swap(
            pick(value, 1 - mine, 1).astype(jnp.bfloat16), axis, bit
        ).astype(jnp.float32)
    return value[0]


def share_rows(value, axis):
    count = lax.axis_size(axis)
    place = lax.axis_index(axis)
    rows, width = value.shape
    value = value[None]
    for bit in reversed(range(count.bit_length() - 1)):
        mine = (place >> bit) & 1
        other = swap(value, axis, bit)
        value = jnp.where(mine == 0, jnp.stack([value, other], 1), jnp.stack([other, value], 1))
        value = value.reshape(-1, rows, width)
    return value.reshape(-1, width)


def gather_columns(value):
    count = value.shape[0] * value.shape[1]
    return value.reshape(count, *value.shape[2:]).transpose(1, 0, 2).reshape(value.shape[2], -1)


def simple_window(local_part):
    tokens = local_part.shape[0]
    shared = lax.all_gather(local_part, "head", axis=1, tiled=True)
    first_pair = shared[:, : 2 * HD]
    second_pair = shared[:, 2 * HD :]
    reach = W1 // tokens
    earlier, rim = from_behind((first_pair, second_pair[tokens - W2 :]), "ctx", 1)
    pieces = [earlier]
    for distance in range(2, reach + 1):
        pieces.append(from_behind(first_pair, "ctx", distance))
    one = jnp.concatenate(pieces[::-1] + [first_pair], 0)
    two = jnp.concatenate([rim, second_pair], 0)
    return one[:, :HD], one[:, HD:], two[:, :HD], two[:, HD:]


def window_of(local_part, source, work):
    done = []

    def beside(values):
        nonlocal source
        if done:
            values, source, done[-1] = lax.optimization_barrier((values, source, done[-1]))
        done.append(work[len(done)](source))
        return values

    tokens = local_part.shape[0]
    heads = lax.axis_size("head")
    odd = lax.axis_index("ctx") & 1
    place = lax.axis_index("head")
    if heads < 4 or lax.axis_size("ctx") % 2 or W1 != 4 * tokens:
        return simple_window(local_part), [piece(source) for piece in work]
    value = beside(local_part[None])
    for bit in reversed(range(1, heads.bit_length() - 1)):
        other = swap(value, "head", bit)
        mine = (place >> bit) & 1
        value = jnp.stack([jnp.where(mine == 0, value, other), jnp.where(mine == 0, other, value)], 1)
        value = value.reshape(-1, *local_part.shape)
    half = value.shape[0] // 2
    first, second = value[:half], value[half:]
    rim = second[:, tokens - W2 :]
    first_rim, first = beside((jnp.concatenate([first, rim], 1), first))
    two_back = from_behind(first_rim, "ctx", 2)
    four_back = from_behind(first, "ctx", 4)
    two_back, two_rim = two_back[:, :tokens], two_back[:, tokens:]
    sent = jnp.concatenate([four_back, two_back, first, jnp.where(odd == 0, rim, two_rim)], 1)
    other = swap(beside(sent), "ctx", 0)
    other, done[-1] = lax.optimization_barrier((other, done[-1]))
    far, near, there = (other[:, step * tokens : (step + 1) * tokens] for step in range(3))
    value = jnp.concatenate(
        [
            four_back,
            jnp.where(odd == 0, far, near),
            two_back,
            jnp.where(odd == 0, near, there),
            first,
            other[:, 3 * tokens :],
            second,
        ],
        1,
    )
    other = swap(value, "head", 0)
    mine = place & 1
    value = jnp.stack([jnp.where(mine == 0, value, other), jnp.where(mine == 0, other, value)], 1)
    one, two = value[:, :, : W1 + tokens], value[:, :, W1 + tokens :]
    one, two = gather_columns(one), gather_columns(two)
    return (one[:, :HD], one[:, HD:], two[:, :HD], two[:, HD:]), done


def attention_kernel(
    place, q_first, q_middle, q_last, k1_ref, v1_ref, k2_ref, v2_ref, weight_hbm, kept_ref, sent_ref,
    weight, arrived, attention, query, last_key, first_key, key_diag, value_diag, column, order, result, scores, bound,
    *, count,
):
    tokens = q_first.shape[0]
    share = tokens // count
    blocks = W1 // tokens + 1
    width = q_first.shape[1] + q_middle.shape[1] + q_last.shape[1]
    pairs = width // (2 * HD)
    lines = query.shape[1]
    rows = lines * W2
    rate = HD ** -0.5 * math.log2(math.e)
    slab = place[0]
    side = place[1]

    def twice(x):
        return jnp.concatenate([x, x], axis=-1)

    def diag(x):
        zero = jnp.zeros_like(x)
        return jnp.concatenate(
            [jnp.concatenate([x, zero], axis=1), jnp.concatenate([zero, x], axis=1)], axis=0
        )

    copies = [
        pltpu.make_async_copy(
            weight_hbm.at[pair * 2 * HD:(pair + 1) * 2 * HD], weight.at[pair * 2 * HD:(pair + 1) * 2 * HD],
            arrived.at[pair],
        )
        for pair in range(pairs)
    ]
    for copy in copies:
        copy.start()
    if lines > pairs:
        query[...] = jnp.zeros(query.shape, query.dtype)
    line = 0
    for part in (q_first, q_middle, q_last):
        for lane in range(0, part.shape[1], HD):
            half = line % 2 * HD
            query[:, line // 2, half:half + HD] = part[:, lane:lane + HD].astype(jnp.float32)
            line += 1
    for j in range(blocks):
        there = slice(j * tokens, (j + 1) * tokens)
        key = k1_ref[there, :].T
        if j < blocks - 1:
            value_diag[j] = diag(v1_ref[there, :])
        if j == 0:
            first_key[...] = key
        elif j == blocks - 1:
            last_key[...] = key
        else:
            key_diag[j - 1] = diag(key)
    order[...] = lax.broadcasted_iota(jnp.int32, order.shape, 0).astype(jnp.float32).astype(order.dtype)
    column[...] = lax.broadcasted_iota(jnp.int32, column.shape, 1).astype(jnp.float32).astype(column.dtype)

    key = k1_ref[...].astype(jnp.float32)
    longest = jnp.max(jnp.sum(key * key, axis=1, keepdims=True), axis=0, keepdims=True)
    key = k2_ref[...]
    key = (key * key).astype(jnp.bfloat16)
    row = lax.broadcasted_iota(jnp.int32, (tokens, key.shape[0]), 0)
    col = lax.broadcasted_iota(jnp.int32, (tokens, key.shape[0]), 1)
    seen = (col > row) & (col <= row + W2)
    for pair in range(lines):
        for half in (0, HD):
            line = query[:, pair, half:half + HD]
            size = lax.dot_general(
                (line * line).astype(jnp.bfloat16), key, (((1,), (1,)), ((), ())),
                preferred_element_type=jnp.float32,
            )
            size = jnp.max(jnp.where(seen, size, 0.0), axis=1, keepdims=True)
            size = jnp.sqrt(size * longest) * (1.03 * rate) - HEADROOM
            bound[:, pair, half:half + HD] = jnp.broadcast_to(size, (tokens, HD))

    def used(behind):
        return [0] + list(range(blocks - 1 - behind, blocks - 1))[-(blocks - 2):] if behind else [0]

    def products(position, behind):
        line = query[position]
        line = jnp.concatenate([line] * (16 // lines), axis=0).astype(jnp.bfloat16)
        mixed = []
        for start in range(0, W2, 16 // lines):
            near = [
                jnp.broadcast_to(k2_ref[pl.ds(position + 1 + start + step, 1), :], (lines, HD))
                for step in range(16 // lines)
            ]
            mixed.append(line * twice(jnp.concatenate(near, axis=0).astype(jnp.bfloat16)))
        mixed = jnp.concatenate(mixed, axis=0)
        here = jnp.broadcast_to(position, (16, tokens)).astype(jnp.float32).astype(jnp.bfloat16)
        late = jnp.concatenate([column[...] <= here] * (HD // 16), axis=0)
        if behind < blocks - 1:
            open_from = jnp.where(slab >= blocks - 1, 2 * tokens, position)
            bias = lax.broadcasted_iota(jnp.int32, (1, 2 * tokens), 1) % tokens <= open_from
            bias = jnp.where(bias, 0.0, -jnp.inf)[None]
            if behind * tokens < W2 - 1:
                shown = lax.broadcasted_iota(jnp.int32, (W2, 1, 1), 0) + (position + behind * tokens)
                bias = bias + jnp.where(shown >= W2 - 1, 0.0, -jnp.inf)
        parts = []
        for j in used(behind):
            if j == 0:
                weights = diag(jnp.where(late, last_key[...], first_key[...]))
            else:
                weights = key_diag[j - 1]
            part = jnp.dot(mixed, weights, preferred_element_type=jnp.float32)
            if j == 0 and behind < blocks - 1:
                part = (part.reshape(W2, lines, 2 * tokens) + bias).reshape(part.shape)
            parts.append(part)
        return parts

    def attend(position, behind, parts, shift):
        base = pl.multiple_of(position // 16 * 16, 16)
        far = pl.multiple_of((blocks - 1) * tokens + base, 16)
        late = order[...] <= jnp.broadcast_to(position - base, (16, HD)).astype(jnp.float32).astype(jnp.bfloat16)
        value = jnp.where(late, v1_ref[pl.ds(far, 16), :], v1_ref[pl.ds(base, 16), :])
        value_diag[0, pl.ds(base, 16), :HD] = value
        value_diag[0, pl.ds(pl.multiple_of(tokens + base, 16), 16), HD:] = value
        blended = total = None
        for j, part in zip(used(behind), parts):
            part = part.reshape(W2, lines, 2 * tokens)
            part = jnp.exp2(part * rate - shift[None])
            add = jnp.sum(part, axis=0)
            total = add if total is None else total + add
            part = jnp.dot(
                part.reshape(rows, 2 * tokens).astype(jnp.bfloat16), value_diag[j],
                preferred_element_type=jnp.float32,
            )
            blended = part if blended is None else blended + part
        acc = None
        for step in range(W2):
            near = jnp.broadcast_to(v2_ref[pl.ds(position + 1 + step, 1), :], (lines, HD))
            part = twice(near) * blended[step * lines:(step + 1) * lines]
            acc = part if acc is None else acc + part
        left = jnp.sum(total[:, :tokens], axis=1, keepdims=True)
        right = jnp.sum(total[:, tokens:], axis=1, keepdims=True)
        result[position] = jnp.concatenate([acc[:, :HD] / left, acc[:, HD:] / right], axis=1)
        return jnp.broadcast_to(jnp.minimum(left, right), (lines, HD))

    def exact(behind, position, _):
        peak = None
        for j, part in zip(used(behind), products(position, behind)):
            scores[j] = part
            high = jnp.max(part.reshape(W2, lines, 2 * tokens), axis=0)
            peak = high if peak is None else jnp.maximum(peak, high)
        left = jnp.max(peak[:, :tokens], axis=1, keepdims=True) * rate
        right = jnp.max(peak[:, tokens:], axis=1, keepdims=True) * rate
        shift = jnp.concatenate(
            [jnp.broadcast_to(left, (lines, tokens)), jnp.broadcast_to(right, (lines, tokens))], axis=1
        )
        attend(position, behind, [scores[j] for j in used(behind)], shift)
        return 0

    def run(behind):
        group = GROUP if len(used(behind)) == blocks - 1 else SHORT_GROUP

        def trip(index, low):
            for step in range(group):
                position = index * group + step
                low = jnp.minimum(low, attend(position, behind, products(position, behind), bound[position]))
            return low

        low = lax.fori_loop(0, tokens // group, trip, jnp.full((lines, HD), jnp.inf, jnp.float32))
        kept_all = jnp.min(low) >= FLOOR

        @pl.when(jnp.logical_not(kept_all))
        def _():
            value_diag[0] = diag(v1_ref[:tokens, :])
            lax.fori_loop(0, tokens, functools.partial(exact, behind), 0)

    for behind in range(blocks - 1):
        pl.when(jnp.minimum(slab, blocks - 2) == behind)(functools.partial(run, behind))

    for pair in range(pairs):
        attention[:, pair * 2 * HD:(pair + 1) * 2 * HD] = result[:, pair, :].astype(attention.dtype)
    for copy in copies:
        copy.wait()
    step = min(1024, weight.shape[1])
    for lane in range(0, weight.shape[1], step):
        product = jnp.dot(
            attention[...], weight[:, lane:lane + step], preferred_element_type=jnp.float32
        ).reshape(-1, 2, share, step)
        even, odd = product[:, 0], product[:, 1]
        kept = jnp.where(side == 0, even, odd)
        sent = jnp.where(side == 0, odd, even)
        kept_ref[:, lane:lane + step] = kept.reshape(-1, step)
        sent_ref[:, lane:lane + step] = sent.reshape(-1, step).astype(sent_ref.dtype)


def share_kernel(source_hbm, weight_hbm, source, out, weight, arrived):
    size = weight.shape[0] // PIECES
    rows = [slice(step * size, (step + 1) * size) for step in range(PIECES)]
    copies = [
        (
            pltpu.make_async_copy(source_hbm.at[:, part], source.at[:, part], arrived.at[0, step]),
            pltpu.make_async_copy(weight_hbm.at[part], weight.at[part], arrived.at[1, step]),
        )
        for step, part in enumerate(rows)
    ]
    for one, two in copies:
        one.start()
        two.start()
    product = None
    for (one, two), part in zip(copies, rows):
        one.wait()
        two.wait()
        add = jnp.dot(source[:, part], weight[part, :], preferred_element_type=jnp.float32)
        product = add if product is None else product + add
    out[...] = product.astype(out.dtype)


def share(source, weight):
    vmem = pl.BlockSpec(memory_space=pltpu.VMEM)
    return pl.pallas_call(
        share_kernel,
        out_shape=(
            jax.ShapeDtypeStruct(source.shape, source.dtype),
            jax.ShapeDtypeStruct((source.shape[0], weight.shape[1]), jnp.bfloat16),
        ),
        in_specs=[pl.BlockSpec(memory_space=pl.ANY)] * 2,
        out_specs=(vmem, vmem),
        scratch_shapes=[pltpu.VMEM(weight.shape, weight.dtype), pltpu.SemaphoreType.DMA((2, PIECES))],
        compiler_params=pltpu.CompilerParams(vmem_limit_bytes=8 * 1024 * 1024),
        name="share",
    )(pltpu.with_memory_space_constraint(source, pltpu.HBM), pltpu.with_memory_space_constraint(weight, pltpu.HBM))


def project_kernel(source, weight_hbm, out, weight, arrived, *, lane):
    width = out.shape[1]
    size = weight.shape[0] // PIECES
    rows = [slice(step * size, (step + 1) * size) for step in range(PIECES)]
    copies = [
        pltpu.make_async_copy(weight_hbm.at[part, lane:lane + width], weight.at[part], arrived.at[step])
        for step, part in enumerate(rows)
    ]
    for copy in copies:
        copy.start()
    product = None
    for copy, part in zip(copies, rows):
        copy.wait()
        add = jnp.dot(source[:, part], weight[part, :], preferred_element_type=jnp.float32)
        product = add if product is None else product + add
    out[...] = product.astype(out.dtype)


def project(weight, lane, width, source):
    vmem = pl.BlockSpec(memory_space=pltpu.VMEM)
    return pl.pallas_call(
        functools.partial(project_kernel, lane=lane),
        out_shape=jax.ShapeDtypeStruct((source.shape[0], width), jnp.bfloat16),
        in_specs=[vmem, pl.BlockSpec(memory_space=pl.ANY)],
        out_specs=vmem,
        scratch_shapes=[
            pltpu.VMEM((weight.shape[0], width), weight.dtype), pltpu.SemaphoreType.DMA((PIECES,)),
        ],
        compiler_params=pltpu.CompilerParams(vmem_limit_bytes=16 * 1024 * 1024),
        cost_estimate=pl.CostEstimate(
            flops=2 * source.shape[0] * weight.shape[0] * width,
            bytes_accessed=2 * weight.shape[0] * width,
            transcendentals=0,
        ),
        name="project",
    )(source, weight)


def attention_of(place, count, queries, key_one, value_one, key_two, value_two, out_weight):
    tokens = queries[0].shape[0]
    width = out_weight.shape[0]
    blocks = W1 // tokens + 1
    pairs = width // (2 * HD)
    lines = -(-pairs // 8) * 8
    rows = lines * W2
    vmem = pl.BlockSpec(memory_space=pltpu.VMEM)
    return pl.pallas_call(
        functools.partial(attention_kernel, count=count),
        out_shape=(
            jax.ShapeDtypeStruct((tokens // 2, out_weight.shape[1]), jnp.float32),
            jax.ShapeDtypeStruct((tokens // 2, out_weight.shape[1]), jnp.bfloat16),
        ),
        in_specs=[pl.BlockSpec(memory_space=pltpu.SMEM)] + [vmem] * 7 + [pl.BlockSpec(memory_space=pl.ANY)],
        out_specs=(vmem, vmem),
        scratch_shapes=[
            pltpu.VMEM(out_weight.shape, out_weight.dtype),
            pltpu.SemaphoreType.DMA((pairs,)),
            pltpu.VMEM((tokens, width), jnp.bfloat16),
            pltpu.VMEM((tokens, lines, 2 * HD), jnp.float32),
            pltpu.VMEM((HD, tokens), jnp.bfloat16),
            pltpu.VMEM((HD, tokens), jnp.bfloat16),
            pltpu.VMEM((blocks - 2, 2 * HD, 2 * tokens), jnp.bfloat16),
            pltpu.VMEM((blocks - 1, 2 * tokens, 2 * HD), jnp.bfloat16),
            pltpu.VMEM((16, tokens), jnp.bfloat16),
            pltpu.VMEM((16, HD), jnp.bfloat16),
            pltpu.VMEM((tokens, lines, 2 * HD), jnp.float32),
            pltpu.VMEM((blocks - 1, rows, 2 * tokens), jnp.float32),
            pltpu.VMEM((tokens, lines, 2 * HD), jnp.float32),
        ],
        compiler_params=pltpu.CompilerParams(vmem_limit_bytes=40 * 1024 * 1024),
        name="attention",
    )(
        place,
        *queries,
        key_one,
        value_one,
        key_two.astype(jnp.float32),
        value_two.astype(jnp.float32),
        out_weight,
    )


def body(hidden_in, query_weight, shared_weight, out_weight, residual, norm_gain):
    source, local_part = share(hidden_in, shared_weight)
    half = query_weight.shape[1] // 2
    query_weight = pltpu.with_memory_space_constraint(query_weight, pltpu.HBM)
    window, queries = window_of(
        local_part,
        source,
        [
            functools.partial(project, query_weight, lane, width)
            for lane, width in ((0, half // 2), (half // 2, half), (half // 2 + half, half // 2))
        ],
    )
    place = jnp.stack([lax.axis_index("ctx"), lax.axis_index("head") & 1]).astype(jnp.int32)
    kept, sent = attention_of(place, lax.axis_size("head"), queries, *window, out_weight)
    summed = sum_to_owner(kept, sent, "head")
    residual_out = (residual.astype(jnp.float32) + summed).astype(jnp.bfloat16)
    values = residual_out.astype(jnp.float32)
    scale = lax.rsqrt(jnp.mean(values * values, axis=1, keepdims=True) + 1e-05)
    normed_local = (values * scale * norm_gain).astype(jnp.bfloat16)
    normed = share_rows(normed_local, "head")
    return (residual_out, normed)


def solution(mesh):
    in_specs = (
        P("ctx", None),
        P(None, "head"),
        P(None, "head"),
        P("head", None),
        P(("ctx", "head"), None),
        P(),
    )
    out_specs = (P(("ctx", "head"), None), P("ctx", None))
    return jax.shard_map(body, mesh=mesh, in_specs=in_specs, out_specs=out_specs, check_vma=False)
```

```python
import functools
import math

import jax
import jax.numpy as jnp
from jax import lax
from jax.experimental import pallas as pl
from jax.experimental.pallas import tpu as pltpu
from jax.sharding import PartitionSpec as P

HD = 128
W1 = 512
W2 = 32
GROUP = 32
SHORT_GROUP = 8
HEADROOM = 60.0
FLOOR = 2.0 ** -88
PIECES = 4


def from_behind(value, axis, steps):
    count = lax.axis_size(axis)
    initial, last = (max(0, -steps), min(count, count - steps))
    return lax.ppermute(value, axis, [(source, source + steps) for source in range(initial, last)])


def swap(value, axis, bit):
    count = lax.axis_size(axis)
    return lax.ppermute(value, axis, [(source, source ^ (1 << bit)) for source in range(count)])


def pick(value, place, dim):
    return lax.dynamic_index_in_dim(value, place, dim, keepdims=False)


def sum_to_owner(kept, sent, axis):
    count = lax.axis_size(axis)
    place = lax.axis_index(axis)
    value = kept + swap(sent, axis, 0).astype(jnp.float32)
    value = value.reshape(count // 2, -1, value.shape[1])
    for bit in range(1, count.bit_length() - 1):
        value = value.reshape(value.shape[0] // 2, 2, *value.shape[1:])
        mine = (place >> bit) & 1
        value = pick(value, mine, 1) + swap(
            pick(value, 1 - mine, 1).astype(jnp.bfloat16), axis, bit
        ).astype(jnp.float32)
    return value[0]


def share_rows(value, axis):
    count = lax.axis_size(axis)
    place = lax.axis_index(axis)
    rows, width = value.shape
    value = value[None]
    for bit in reversed(range(count.bit_length() - 1)):
        mine = (place >> bit) & 1
        other = swap(value, axis, bit)
        value = jnp.where(mine == 0, jnp.stack([value, other], 1), jnp.stack([other, value], 1))
        value = value.reshape(-1, rows, width)
    return value.reshape(-1, width)


def gather_columns(value):
    count = value.shape[0] * value.shape[1]
    return value.reshape(count, *value.shape[2:]).transpose(1, 0, 2).reshape(value.shape[2], -1)


def simple_window(local_part):
    tokens = local_part.shape[0]
    shared = lax.all_gather(local_part, "head", axis=1, tiled=True)
    first_pair = shared[:, : 2 * HD]
    second_pair = shared[:, 2 * HD :]
    reach = W1 // tokens
    earlier, rim = from_behind((first_pair, second_pair[tokens - W2 :]), "ctx", 1)
    pieces = [earlier]
    for distance in range(2, reach + 1):
        pieces.append(from_behind(first_pair, "ctx", distance))
    one = jnp.concatenate(pieces[::-1] + [first_pair], 0)
    two = jnp.concatenate([rim, second_pair], 0)
    return one[:, :HD], one[:, HD:], two[:, :HD], two[:, HD:]


def window_of(local_part, source, work):
    done = []

    def beside(values):
        nonlocal source
        if done:
            values, source, done[-1] = lax.optimization_barrier((values, source, done[-1]))
        done.append(work[len(done)](source))
        return values

    tokens = local_part.shape[0]
    heads = lax.axis_size("head")
    odd = lax.axis_index("ctx") & 1
    place = lax.axis_index("head")
    if heads < 4 or lax.axis_size("ctx") % 2 or W1 != 4 * tokens:
        return simple_window(local_part), [piece(source) for piece in work]
    value = beside(local_part[None])
    for bit in reversed(range(1, heads.bit_length() - 1)):
        other = swap(value, "head", bit)
        mine = (place >> bit) & 1
        value = jnp.stack([jnp.where(mine == 0, value, other), jnp.where(mine == 0, other, value)], 1)
        value = value.reshape(-1, *local_part.shape)
    half = value.shape[0] // 2
    first, second = value[:half], value[half:]
    rim = second[:, tokens - W2 :]
    first_rim, first = beside((jnp.concatenate([first, rim], 1), first))
    two_back = from_behind(first_rim, "ctx", 2)
    four_back = from_behind(first, "ctx", 4)
    two_back, two_rim = two_back[:, :tokens], two_back[:, tokens:]
    sent = jnp.concatenate([four_back, two_back, first, jnp.where(odd == 0, rim, two_rim)], 1)
    other = swap(beside(sent), "ctx", 0)
    other, done[-1] = lax.optimization_barrier((other, done[-1]))
    far, near, there = (other[:, step * tokens : (step + 1) * tokens] for step in range(3))
    value = jnp.concatenate(
        [
            four_back,
            jnp.where(odd == 0, far, near),
            two_back,
            jnp.where(odd == 0, near, there),
            first,
            other[:, 3 * tokens :],
            second,
        ],
        1,
    )
    other = swap(value, "head", 0)
    mine = place & 1
    value = jnp.stack([jnp.where(mine == 0, value, other), jnp.where(mine == 0, other, value)], 1)
    one, two = value[:, :, : W1 + tokens], value[:, :, W1 + tokens :]
    one, two = gather_columns(one), gather_columns(two)
    return (one[:, :HD], one[:, HD:], two[:, :HD], two[:, HD:]), done


def attention_kernel(
    place, q_first, q_middle, q_last, k1_ref, v1_ref, k2_ref, v2_ref, weight_hbm, kept_ref, sent_ref,
    weight, arrived, attention, query, last_key, first_key, key_diag, value_diag, column, order, result, scores, bound,
    *, count,
):
    tokens = q_first.shape[0]
    share = tokens // count
    blocks = W1 // tokens + 1
    width = q_first.shape[1] + q_middle.shape[1] + q_last.shape[1]
    pairs = width // (2 * HD)
    lines = query.shape[1]
    rows = lines * W2
    rate = HD ** -0.5 * math.log2(math.e)
    slab = place[0]
    side = place[1]

    def twice(x):
        return jnp.concatenate([x, x], axis=-1)

    def diag(x):
        zero = jnp.zeros_like(x)
        return jnp.concatenate(
            [jnp.concatenate([x, zero], axis=1), jnp.concatenate([zero, x], axis=1)], axis=0
        )

    copies = [
        pltpu.make_async_copy(
            weight_hbm.at[pair * 2 * HD:(pair + 1) * 2 * HD], weight.at[pair * 2 * HD:(pair + 1) * 2 * HD],
            arrived.at[pair],
        )
        for pair in range(pairs)
    ]
    for copy in copies:
        copy.start()
    if lines > pairs:
        query[...] = jnp.zeros(query.shape, query.dtype)
    line = 0
    for part in (q_first, q_middle, q_last):
        for lane in range(0, part.shape[1], HD):
            half = line % 2 * HD
            query[:, line // 2, half:half + HD] = part[:, lane:lane + HD].astype(jnp.float32)
            line += 1
    for j in range(blocks):
        there = slice(j * tokens, (j + 1) * tokens)
        key = k1_ref[there, :].T
        if j < blocks - 1:
            value_diag[j] = diag(v1_ref[there, :])
        if j == 0:
            first_key[...] = key
        elif j == blocks - 1:
            last_key[...] = key
        else:
            key_diag[j - 1] = diag(key)
    order[...] = lax.broadcasted_iota(jnp.int32, order.shape, 0).astype(jnp.float32).astype(order.dtype)
    column[...] = lax.broadcasted_iota(jnp.int32, column.shape, 1).astype(jnp.float32).astype(column.dtype)

    key = k1_ref[...].astype(jnp.float32)
    longest = jnp.max(jnp.sum(key * key, axis=1, keepdims=True), axis=0, keepdims=True)
    key = k2_ref[...]
    key = (key * key).astype(jnp.bfloat16)
    row = lax.broadcasted_iota(jnp.int32, (tokens, key.shape[0]), 0)
    col = lax.broadcasted_iota(jnp.int32, (tokens, key.shape[0]), 1)
    seen = (col > row) & (col <= row + W2)
    for pair in range(lines):
        for half in (0, HD):
            line = query[:, pair, half:half + HD]
            size = lax.dot_general(
                (line * line).astype(jnp.bfloat16), key, (((1,), (1,)), ((), ())),
                preferred_element_type=jnp.float32,
            )
            size = jnp.max(jnp.where(seen, size, 0.0), axis=1, keepdims=True)
            size = jnp.sqrt(size * longest) * (1.03 * rate) - HEADROOM
            bound[:, pair, half:half + HD] = jnp.broadcast_to(size, (tokens, HD))

    def used(behind):
        return [0] + list(range(blocks - 1 - behind, blocks - 1))[-(blocks - 2):] if behind else [0]

    def products(position, behind):
        line = query[position]
        line = jnp.concatenate([line] * (16 // lines), axis=0).astype(jnp.bfloat16)
        mixed = []
        for start in range(0, W2, 16 // lines):
            near = [
                jnp.broadcast_to(k2_ref[pl.ds(position + 1 + start + step, 1), :], (lines, HD))
                for step in range(16 // lines)
            ]
            mixed.append(line * twice(jnp.concatenate(near, axis=0).astype(jnp.bfloat16)))
        mixed = jnp.concatenate(mixed, axis=0)
        here = jnp.broadcast_to(position, (16, tokens)).astype(jnp.float32).astype(jnp.bfloat16)
        late = jnp.concatenate([column[...] <= here] * (HD // 16), axis=0)
        if behind < blocks - 1:
            open_from = jnp.where(slab >= blocks - 1, 2 * tokens, position)
            bias = lax.broadcasted_iota(jnp.int32, (1, 2 * tokens), 1) % tokens <= open_from
            bias = jnp.where(bias, 0.0, -jnp.inf)[None]
            if behind * tokens < W2 - 1:
                shown = lax.broadcasted_iota(jnp.int32, (W2, 1, 1), 0) + (position + behind * tokens)
                bias = bias + jnp.where(shown >= W2 - 1, 0.0, -jnp.inf)
        parts = []
        for j in used(behind):
            if j == 0:
                weights = diag(jnp.where(late, last_key[...], first_key[...]))
            else:
                weights = key_diag[j - 1]
            part = jnp.dot(mixed, weights, preferred_element_type=jnp.float32)
            if j == 0 and behind < blocks - 1:
                part = (part.reshape(W2, lines, 2 * tokens) + bias).reshape(part.shape)
            parts.append(part)
        return parts

    def attend(position, behind, parts, shift):
        base = pl.multiple_of(position // 16 * 16, 16)
        far = pl.multiple_of((blocks - 1) * tokens + base, 16)
        late = order[...] <= jnp.broadcast_to(position - base, (16, HD)).astype(jnp.float32).astype(jnp.bfloat16)
        value = jnp.where(late, v1_ref[pl.ds(far, 16), :], v1_ref[pl.ds(base, 16), :])
        value_diag[0, pl.ds(base, 16), :HD] = value
        value_diag[0, pl.ds(pl.multiple_of(tokens + base, 16), 16), HD:] = value
        blended = total = None
        for j, part in zip(used(behind), parts):
            part = part.reshape(W2, lines, 2 * tokens)
            part = jnp.exp2(part * rate - shift[None])
            add = jnp.sum(part, axis=0)
            total = add if total is None else total + add
            part = jnp.dot(
                part.reshape(rows, 2 * tokens).astype(jnp.bfloat16), value_diag[j],
                preferred_element_type=jnp.float32,
            )
            blended = part if blended is None else blended + part
        acc = None
        for step in range(W2):
            near = jnp.broadcast_to(v2_ref[pl.ds(position + 1 + step, 1), :], (lines, HD))
            part = twice(near) * blended[step * lines:(step + 1) * lines]
            acc = part if acc is None else acc + part
        left = jnp.sum(total[:, :tokens], axis=1, keepdims=True)
        right = jnp.sum(total[:, tokens:], axis=1, keepdims=True)
        result[position] = jnp.concatenate([acc[:, :HD] / left, acc[:, HD:] / right], axis=1)
        return jnp.broadcast_to(jnp.minimum(left, right), (lines, HD))

    def exact(behind, position, _):
        peak = None
        for j, part in zip(used(behind), products(position, behind)):
            scores[j] = part
            high = jnp.max(part.reshape(W2, lines, 2 * tokens), axis=0)
            peak = high if peak is None else jnp.maximum(peak, high)
        left = jnp.max(peak[:, :tokens], axis=1, keepdims=True) * rate
        right = jnp.max(peak[:, tokens:], axis=1, keepdims=True) * rate
        shift = jnp.concatenate(
            [jnp.broadcast_to(left, (lines, tokens)), jnp.broadcast_to(right, (lines, tokens))], axis=1
        )
        attend(position, behind, [scores[j] for j in used(behind)], shift)
        return 0

    def run(behind):
        group = GROUP if len(used(behind)) == blocks - 1 else SHORT_GROUP

        def trip(index, low):
            for step in range(group):
                position = index * group + step
                low = jnp.minimum(low, attend(position, behind, products(position, behind), bound[position]))
            return low

        low = lax.fori_loop(0, tokens // group, trip, jnp.full((lines, HD), jnp.inf, jnp.float32))
        kept_all = jnp.min(low) >= FLOOR

        @pl.when(jnp.logical_not(kept_all))
        def _():
            value_diag[0] = diag(v1_ref[:tokens, :])
            lax.fori_loop(0, tokens, functools.partial(exact, behind), 0)

    for behind in range(blocks - 1):
        pl.when(jnp.minimum(slab, blocks - 2) == behind)(functools.partial(run, behind))

    for pair in range(pairs):
        attention[:, pair * 2 * HD:(pair + 1) * 2 * HD] = result[:, pair, :].astype(attention.dtype)
    for copy in copies:
        copy.wait()
    step = min(1024, weight.shape[1])
    for lane in range(0, weight.shape[1], step):
        product = jnp.dot(
            attention[...], weight[:, lane:lane + step], preferred_element_type=jnp.float32
        ).reshape(-1, 2, share, step)
        even, odd = product[:, 0], product[:, 1]
        kept = jnp.where(side == 0, even, odd)
        sent = jnp.where(side == 0, odd, even)
        kept_ref[:, lane:lane + step] = kept.reshape(-1, step)
        sent_ref[:, lane:lane + step] = sent.reshape(-1, step).astype(sent_ref.dtype)


def share_kernel(source_hbm, weight_hbm, source, out, weight, arrived):
    size = weight.shape[0] // PIECES
    rows = [slice(step * size, (step + 1) * size) for step in range(PIECES)]
    copies = [
        (
            pltpu.make_async_copy(source_hbm.at[:, part], source.at[:, part], arrived.at[0, step]),
            pltpu.make_async_copy(weight_hbm.at[part], weight.at[part], arrived.at[1, step]),
        )
        for step, part in enumerate(rows)
    ]
    for one, two in copies:
        one.start()
        two.start()
    product = None
    for (one, two), part in zip(copies, rows):
        one.wait()
        two.wait()
        add = jnp.dot(source[:, part], weight[part, :], preferred_element_type=jnp.float32)
        product = add if product is None else product + add
    out[...] = product.astype(out.dtype)


def share(source, weight):
    vmem = pl.BlockSpec(memory_space=pltpu.VMEM)
    return pl.pallas_call(
        share_kernel,
        out_shape=(
            jax.ShapeDtypeStruct(source.shape, source.dtype),
            jax.ShapeDtypeStruct((source.shape[0], weight.shape[1]), jnp.bfloat16),
        ),
        in_specs=[pl.BlockSpec(memory_space=pl.ANY)] * 2,
        out_specs=(vmem, vmem),
        scratch_shapes=[pltpu.VMEM(weight.shape, weight.dtype), pltpu.SemaphoreType.DMA((2, PIECES))],
        compiler_params=pltpu.CompilerParams(vmem_limit_bytes=8 * 1024 * 1024),
        name="share",
    )(pltpu.with_memory_space_constraint(source, pltpu.HBM), pltpu.with_memory_space_constraint(weight, pltpu.HBM))


def project_kernel(source, weight_hbm, out, weight, arrived, *, lane):
    width = out.shape[1]
    size = weight.shape[0] // PIECES
    rows = [slice(step * size, (step + 1) * size) for step in range(PIECES)]
    copies = [
        pltpu.make_async_copy(weight_hbm.at[part, lane:lane + width], weight.at[part], arrived.at[step])
        for step, part in enumerate(rows)
    ]
    for copy in copies:
        copy.start()
    product = None
    for copy, part in zip(copies, rows):
        copy.wait()
        add = jnp.dot(source[:, part], weight[part, :], preferred_element_type=jnp.float32)
        product = add if product is None else product + add
    out[...] = product.astype(out.dtype)


def project(weight, lane, width, source):
    vmem = pl.BlockSpec(memory_space=pltpu.VMEM)
    return pl.pallas_call(
        functools.partial(project_kernel, lane=lane),
        out_shape=jax.ShapeDtypeStruct((source.shape[0], width), jnp.bfloat16),
        in_specs=[vmem, pl.BlockSpec(memory_space=pl.ANY)],
        out_specs=vmem,
        scratch_shapes=[
            pltpu.VMEM((weight.shape[0], width), weight.dtype), pltpu.SemaphoreType.DMA((PIECES,)),
        ],
        compiler_params=pltpu.CompilerParams(vmem_limit_bytes=16 * 1024 * 1024),
        cost_estimate=pl.CostEstimate(
            flops=2 * source.shape[0] * weight.shape[0] * width,
            bytes_accessed=2 * weight.shape[0] * width,
            transcendentals=0,
        ),
        name="project",
    )(source, weight)


def attention_of(place, count, queries, key_one, value_one, key_two, value_two, out_weight):
    tokens = queries[0].shape[0]
    width = out_weight.shape[0]
    blocks = W1 // tokens + 1
    pairs = width // (2 * HD)
    lines = -(-pairs // 8) * 8
    rows = lines * W2
    vmem = pl.BlockSpec(memory_space=pltpu.VMEM)
    return pl.pallas_call(
        functools.partial(attention_kernel, count=count),
        out_shape=(
            jax.ShapeDtypeStruct((tokens // 2, out_weight.shape[1]), jnp.float32),
            jax.ShapeDtypeStruct((tokens // 2, out_weight.shape[1]), jnp.bfloat16),
        ),
        in_specs=[pl.BlockSpec(memory_space=pltpu.SMEM)] + [vmem] * 7 + [pl.BlockSpec(memory_space=pl.ANY)],
        out_specs=(vmem, vmem),
        scratch_shapes=[
            pltpu.VMEM(out_weight.shape, out_weight.dtype),
            pltpu.SemaphoreType.DMA((pairs,)),
            pltpu.VMEM((tokens, width), jnp.bfloat16),
            pltpu.VMEM((tokens, lines, 2 * HD), jnp.float32),
            pltpu.VMEM((HD, tokens), jnp.bfloat16),
            pltpu.VMEM((HD, tokens), jnp.bfloat16),
            pltpu.VMEM((blocks - 2, 2 * HD, 2 * tokens), jnp.bfloat16),
            pltpu.VMEM((blocks - 1, 2 * tokens, 2 * HD), jnp.bfloat16),
            pltpu.VMEM((16, tokens), jnp.bfloat16),
            pltpu.VMEM((16, HD), jnp.bfloat16),
            pltpu.VMEM((tokens, lines, 2 * HD), jnp.float32),
            pltpu.VMEM((blocks - 1, rows, 2 * tokens), jnp.float32),
            pltpu.VMEM((tokens, lines, 2 * HD), jnp.float32),
        ],
        compiler_params=pltpu.CompilerParams(vmem_limit_bytes=40 * 1024 * 1024),
        name="attention",
    )(
        place,
        *queries,
        key_one,
        value_one,
        key_two.astype(jnp.float32),
        value_two.astype(jnp.float32),
        out_weight,
    )


def body(hidden_in, query_weight, shared_weight, out_weight, residual, norm_gain):
    source, local_part = share(hidden_in, shared_weight)
    half = query_weight.shape[1] // 2
    query_weight = pltpu.with_memory_space_constraint(query_weight, pltpu.HBM)
    window, queries = window_of(
        local_part,
        source,
        [
            functools.partial(project, query_weight, lane, width)
            for lane, width in ((0, half // 2), (half // 2, half), (half // 2 + half, half // 2))
        ],
    )
    place = jnp.stack([lax.axis_index("ctx"), lax.axis_index("head") & 1]).astype(jnp.int32)
    kept, sent = attention_of(place, lax.axis_size("head"), queries, *window, out_weight)
    summed = sum_to_owner(kept, sent, "head")
    residual_out = (residual.astype(jnp.float32) + summed).astype(jnp.bfloat16)
    values = residual_out.astype(jnp.float32)
    scale = lax.rsqrt(jnp.mean(values * values, axis=1, keepdims=True) + 1e-05)
    normed_local = (values * scale * norm_gain).astype(jnp.bfloat16)
    normed = share_rows(normed_local, "head")
    return (residual_out, normed)


def solution(mesh):
    in_specs = (
        P("ctx", None),
        P(None, "head"),
        P(None, "head"),
        P("head", None),
        P(("ctx", "head"), None),
        P(),
    )
    out_specs = (P(("ctx", "head"), None), P("ctx", None))
    return jax.shard_map(body, mesh=mesh, in_specs=in_specs, out_specs=out_specs, check_vma=False)
```
